32 devices in a mesh: groups: 2 (over x), frames: 16 (over z, y, core).
Axes of the slice: x: 2, y: 2, z: 4, core: 2. Of those that a mesh axis runs over, the one named last changes fastest.
Arguments:
- latents: bfloat16 [256, 32, 512], P(('groups', 'frames')), parts along dimension 0, may hold values from -6 to 6
- timestep: int32 [256], P(('groups', 'frames')), parts along dimension 0, may hold values from 0 to 49, as said below
- lookback: int32 [256], P(('groups', 'frames')), parts along dimension 0, may hold values from 1 to 8, as said below
- modulation: bfloat16 [2, 50, 4, 512], replicated, may hold values from -2.390625 to 2.390625
- input_weight: bfloat16 [2, 512, 2304], replicated, may hold values from -0.25 to 0.25
- step_weight: bfloat16 [2, 512, 16], replicated, may hold values from -0.25 to 0.25
- conv_weight: float32 [2, 4, 1280], replicated, may hold values from -3 to 3
- step_bias: float32 [2, 50, 16], replicated, may hold values from -3 to 2
- decay_log: float32 [2, 16], replicated
- skip_gain: float32 [2, 16], replicated, may hold values from -2 to 2
- norm_gain: float32 [2, 1024], replicated, may hold values from 0.1 to 1.9
- output_weight: bfloat16 [2, 1024, 512], replicated, may hold values from -0.1875 to 0.1875
- query_weight: bfloat16 [2, 512, 512], replicated
- memory_weight: bfloat16 [2, 512, 1024], replicated
- merge_weight: bfloat16 [2, 512, 512], replicated, may hold values from -0.25 to 0.25
Outputs:
- denoised: float32 [256, 32, 512], P(('groups', 'frames')), parts along dimension 0
The draws below stay inside these ranges and needn't reach their ends.
There are 2 independent parts, one for each index of `groups`. The reference program is written for one: setup_inputs(seed, part) draws one part's arguments, and reference() takes and returns one part's arrays. A program takes and returns all parts, laid end to end along the dimension named above; an argument that names none is the same for every part. Nothing has to cross between parts.
Inputs may be any that keep to these rules, and one draw needn't show every extreme that they name: timestep is the same for all frames of each aligned run of 8 frames. lookback[f] counts the preceding frames that frame f attends to; 8 occurs in every draw.
All inputs are finite; a program needn't handle non-finite values.
Results may differ from the reference program's by a relative error of at most 0.01.
Values may be sent and summed in bfloat16 or wider, within the bound.
A program may use at most 128 MiB of HBM per device.

```python
import math
import jax
import jax.numpy as jnp
from jax import lax

D = 512
HEADS = 16
HEAD_DIM = 64
STATE = 128
ATT_HEADS = 8
NSTEPS = 50
LAYERS = 2
CONV = 4
SPAN = 128
WINDOW = 8
TPF = 32
INNER = 1024
ATTN = 512
FRAMES = 128
TOKENS = 4096


def draw_timestep(key, part):
    groups = jax.random.randint(key, (FRAMES // WINDOW,), 0, NSTEPS)
    return jnp.repeat(groups, WINDOW).astype(jnp.int32)


def draw_lookback(key, part):
    first_key, second_key = jax.random.split(key)
    counts = jax.random.randint(first_key, (FRAMES,), 1, WINDOW + 1)
    where_full = jax.random.randint(second_key, (), 0, FRAMES)
    return counts.at[where_full].set(WINDOW).astype(jnp.int32)


def draw_decay_log(key, part):
    ranks = jnp.stack([jax.random.permutation(jax.random.fold_in(key, 11 + layer), HEADS) for layer in range(LAYERS)])
    fast_count = HEADS // 2
    slow_rate = jnp.exp(jax.random.uniform(jax.random.fold_in(key, 1), (LAYERS, HEADS), jnp.float32, math.log(0.7), math.log(2.5))) / TOKENS
    fast_rate = jax.random.uniform(jax.random.fold_in(key, 2), (LAYERS, HEADS), jnp.float32, 0.6, 1.5) / 32.0
    return jnp.log(jnp.where(ranks < fast_count, fast_rate, slow_rate)).astype(jnp.float32)


def key_columns(key):
    return jax.random.normal(jax.random.fold_in(key, 7), (LAYERS, D, ATT_HEADS * HEAD_DIM), jnp.float32) * D ** (-0.5)


def draw_memory_weight(key, part):
    value_part = jax.random.normal(jax.random.fold_in(key, 8), (LAYERS, D, ATT_HEADS * HEAD_DIM), jnp.float32) * D ** (-0.5)
    return jnp.concatenate([key_columns(key), value_part], axis=2).astype(jnp.bfloat16)


def draw_query_weight(key, part):
    values = jax.random.normal(jax.random.fold_in(key, 9), (LAYERS, D, ATT_HEADS * HEAD_DIM), jnp.float32) * D ** (-0.5)
    return values.astype(jnp.bfloat16)


def levels(rng, dims, shards, least, largest):
    def one(dim, parts):
        steps = jax.random.uniform(jax.random.fold_in(jax.random.fold_in(rng, 6), dim), (parts,), jnp.float32, least / len(shards), largest / len(shards))
        return jnp.repeat(jnp.exp(steps), dims[dim] // parts).reshape((-1,) + (1,) * (len(dims) - dim - 1))

    level = one(*shards[0])
    for cut in shards[1:]:
        level = level * one(*cut)
    return level


def normal_values(rng, extent, scale, most, pieces=(), kind=jnp.bfloat16):
    level = levels(rng, extent, pieces, -0.22, 0.18) if pieces else 1.0
    drawn = jax.random.normal(rng, extent, jnp.float32) * scale * level
    return jnp.minimum(jnp.maximum(drawn, -most), most).astype(kind)


def setup_inputs(seed: int = 0, part: int = 0) -> dict:
    streams_of = jax.random.split(jax.random.key(seed), 16)
    part_splits = jax.random.split(jax.random.fold_in(streams_of[15], part), 16)
    return {
        "latents": normal_values(part_splits[0], (FRAMES, TPF, D), 1.0, 6.0, ((0, 16),)),
        "timestep": draw_timestep(jax.random.fold_in(jax.random.fold_in(streams_of[15], part), 71), part),
        "lookback": draw_lookback(jax.random.fold_in(jax.random.fold_in(streams_of[15], part), 71), part),
        "modulation": normal_values(streams_of[3], (LAYERS, NSTEPS, 4, D), 0.4, 2.390625),
        "input_weight": normal_values(streams_of[4], (LAYERS, D, 2 * INNER + 2 * STATE), D ** -0.5, 0.25),
        "step_weight": normal_values(streams_of[5], (LAYERS, D, HEADS), D ** -0.5, 0.25),
        "conv_weight": normal_values(streams_of[6], (LAYERS, CONV, INNER + 2 * STATE), 0.5, 3.0, (), jnp.float32),
        "step_bias": jnp.clip(jax.random.uniform(streams_of[7], (LAYERS, NSTEPS, HEADS), jnp.float32, -3.0, 2.0), -3.0, 2.0),
        "decay_log": draw_decay_log(jax.random.fold_in(streams_of[15], 71), part),
        "skip_gain": jnp.clip(jax.random.uniform(streams_of[9], (LAYERS, HEADS), jnp.float32, -2.0, 2.0), -2.0, 2.0),
        "norm_gain": jnp.clip(1.0 + 0.18 * jax.random.normal(streams_of[10], (LAYERS, INNER), jnp.float32), 0.1, 1.9),
        "output_weight": normal_values(streams_of[11], (LAYERS, INNER, D), INNER ** -0.5, 0.1875),
        "query_weight": draw_query_weight(jax.random.fold_in(streams_of[15], 71), part),
        "memory_weight": draw_memory_weight(jax.random.fold_in(streams_of[15], 71), part),
        "merge_weight": normal_values(streams_of[14], (LAYERS, ATTN, D), ATTN ** -0.5, 0.25),
    }


EPS = 1e-06
HEAD_EPS = 1e-05

def rms_rows(values):
    return values * lax.rsqrt(lax.optimization_barrier(jnp.mean(values * values, axis=-1, keepdims=True)) + EPS)

def modulated(resid, shift, scale):
    normed = rms_rows(resid.astype(jnp.float32))
    return (normed * (1.0 + scale[:, None, :]) + shift[:, None, :]).astype(jnp.bfloat16)

def conv_silu(extended, weights, count):
    total = weights[0][None, :] * extended[0:count].astype(jnp.float32)
    for offset in range(1, CONV):
        total = total + weights[offset][None, :] * extended[offset:offset + count].astype(jnp.float32)
    return jax.nn.silu(total).astype(jnp.bfloat16)

def span_terms(values, input_map, output_map, log_decay, step_size):
    count = values.shape[0] // SPAN
    by_head = values.reshape(count, SPAN, HEADS, HEAD_DIM).astype(jnp.float32)
    in_blocks = input_map.reshape(count, SPAN, STATE).astype(jnp.float32)
    out_blocks = output_map.reshape(count, SPAN, STATE).astype(jnp.float32)
    cumulated = jnp.cumsum(log_decay.reshape(count, SPAN, HEADS), axis=1).transpose(0, 2, 1)
    steps = step_size.reshape(count, SPAN, HEADS).transpose(0, 2, 1)
    affinity = jnp.einsum('cqn,csn->cqs', out_blocks, in_blocks)
    position = jnp.arange(SPAN)
    lower = position[:, None] >= position[None, :]
    gaps = cumulated[:, :, :, None] - cumulated[:, :, None, :]
    gaps = jnp.where(lower[None, None], gaps, -jnp.inf)
    mixing = (affinity[:, None] * jnp.exp(gaps) * steps[:, :, None, :]).astype(jnp.bfloat16)
    y_local = jnp.einsum('chqs,cshp->cqhp', mixing.astype(jnp.float32), by_head)
    edge = jnp.exp(cumulated[:, :, -1:] - cumulated) * steps
    weighted = (in_blocks[:, None, :, :] * edge[:, :, :, None]).astype(jnp.bfloat16)
    states = jnp.einsum('cshp,chsn->chpn', by_head, weighted.astype(jnp.float32))
    return (y_local, states, cumulated, out_blocks)

def finish_mixer(resid, y_total, values, gate_half, skip, gain, weight):
    rows = values.shape[0]
    mixed = y_total.reshape(rows, HEADS * HEAD_DIM) + jnp.repeat(skip, HEAD_DIM)[None, :] * values.astype(jnp.float32)
    gated = (mixed * jax.nn.silu(gate_half.astype(jnp.float32))).reshape(rows, HEADS, HEAD_DIM)
    gated = gated * lax.rsqrt(lax.optimization_barrier(jnp.mean(gated * gated, axis=-1, keepdims=True)) + HEAD_EPS)
    normed = (gated.reshape(rows, HEADS * HEAD_DIM) * gain[None, :]).astype(jnp.bfloat16)
    update = jnp.dot(normed, weight, preferred_element_type=jnp.float32)
    return resid + update.reshape(resid.shape)

def attend(query_block, key_block, query_frame, key_frame, reach):
    count, tok_frame, attn = query_block.shape
    heads = attn // HEAD_DIM
    queries = query_block.reshape(count * tok_frame, heads, HEAD_DIM).astype(jnp.float32)
    key_rows = key_block[:, :, :attn].reshape(-1, heads, HEAD_DIM).astype(jnp.float32)
    value_rows = key_block[:, :, attn:].reshape(-1, heads, HEAD_DIM).astype(jnp.float32)
    scores = jnp.einsum('qhd,khd->hqk', queries, key_rows) * HEAD_DIM ** (-0.5)
    allowed = (key_frame[None, :] >= 0) & (key_frame[None, :] <= query_frame[:, None]) & (key_frame[None, :] >= query_frame[:, None] - reach[:, None])
    allowed = jnp.repeat(jnp.repeat(allowed, tok_frame, axis=0), tok_frame, axis=1)
    scores = jnp.where(allowed[None], scores, -1e+30)
    top = lax.optimization_barrier(jnp.max(scores, axis=-1, keepdims=True))
    weights = jnp.exp(scores - top)
    probs = (weights / lax.optimization_barrier(jnp.sum(weights, axis=-1, keepdims=True))).astype(jnp.bfloat16)
    mixed = jnp.einsum('hqk,khd->qhd', probs.astype(jnp.float32), value_rows)
    return mixed.astype(jnp.bfloat16).reshape(count, tok_frame, attn)

def reference(latents, timestep, lookback, modulation, input_weight, step_weight, conv_weight, step_bias, decay_log, skip_gain, norm_gain, output_weight, query_weight, memory_weight, merge_weight):
    inner = HEADS * HEAD_DIM
    attn = ATT_HEADS * HEAD_DIM
    resid = latents.astype(jnp.float32)
    for layer in range(LAYERS):
        mods = modulation[layer][timestep].astype(jnp.float32)
        frame_bias = step_bias[layer][timestep]
        u_rows = modulated(resid, mods[:, 0], mods[:, 1]).reshape(-1, D)
        projected = jnp.dot(u_rows, input_weight[layer], preferred_element_type=jnp.float32).astype(jnp.bfloat16)
        gate_half = projected[:, :inner]
        mixed_in = projected[:, inner:]
        step_raw = jnp.dot(u_rows, step_weight[layer], preferred_element_type=jnp.float32)
        step_raw = (step_raw.reshape(FRAMES, TPF, HEADS) + frame_bias[:, None, :]).reshape(-1, HEADS)
        extended = jnp.concatenate([jnp.zeros((CONV - 1, mixed_in.shape[1]), jnp.bfloat16), mixed_in], axis=0)
        act = conv_silu(extended, conv_weight[layer], mixed_in.shape[0])
        values = act[:, :inner]
        input_map = act[:, inner:inner + STATE]
        output_map = act[:, inner + STATE:]
        step_size = jax.nn.softplus(step_raw)
        log_decay = -jnp.exp(decay_log[layer])[None, :] * step_size
        y_local, states, cumulated, out_blocks = span_terms(values, input_map, output_map, log_decay, step_size)

        def walk(carry, item):
            state, ends = item
            return (jnp.exp(ends)[:, None, None] * carry + state, carry)
        final_state, before = lax.scan(walk, jnp.zeros((HEADS, HEAD_DIM, STATE), jnp.float32), (states, cumulated[:, :, -1]))
        y_carry = jnp.einsum('cqn,chpn->cqhp', out_blocks, before, precision=lax.Precision.HIGHEST)
        y_carry = y_carry * jnp.exp(cumulated).transpose(0, 2, 1)[:, :, :, None]
        hidden = finish_mixer(resid, y_local + y_carry, values, gate_half, skip_gain[layer], norm_gain[layer], output_weight[layer])
        a_rows = modulated(hidden, mods[:, 2], mods[:, 3]).reshape(-1, D)
        queries = jnp.dot(a_rows, query_weight[layer], preferred_element_type=jnp.float32).astype(jnp.bfloat16).reshape(FRAMES, TPF, attn)
        memory = jnp.dot(a_rows, memory_weight[layer], preferred_element_type=jnp.float32).astype(jnp.bfloat16).reshape(FRAMES, TPF, 2 * attn)
        padded = jnp.concatenate([jnp.zeros((WINDOW, TPF, 2 * attn), jnp.bfloat16), memory], axis=0)

        def one_block(block):
            start = (block * WINDOW).astype(jnp.int32)
            query_block = lax.dynamic_slice_in_dim(queries, start, WINDOW, 0)
            key_block = lax.dynamic_slice_in_dim(padded, start, 2 * WINDOW, 0)
            reach = lax.dynamic_slice_in_dim(lookback, start, WINDOW, 0)
            query_frame = start + jnp.arange(WINDOW, dtype=jnp.int32)
            key_frame = start - WINDOW + jnp.arange(2 * WINDOW, dtype=jnp.int32)
            return attend(query_block, key_block, query_frame, key_frame, reach)
        attended = lax.map(one_block, jnp.arange(FRAMES // WINDOW, dtype=jnp.int32)).reshape(-1, attn)
        update = jnp.dot(attended, merge_weight[layer], preferred_element_type=jnp.float32)
        resid = hidden + update.reshape(hidden.shape)
    return resid
```

```python
import functools

import jax
import jax.numpy as jnp
from jax import lax
from jax.experimental import pallas as pl
from jax.experimental.pallas import tpu as pltpu
from jax.sharding import PartitionSpec as P

HEADS = 16
HEAD_DIM = 64
STATE = 128
ATT_HEADS = 8
LAYERS = 2
CONV = 4
SPAN = 128
WINDOW = 8
EPS = 1e-06
HEAD_EPS = 1e-05
LANES = 128
INNER = HEADS * HEAD_DIM
ATTN = ATT_HEADS * HEAD_DIM
PAIRS = INNER // LANES
F32 = jnp.float32
BF16 = jnp.bfloat16
HIGH = lax.Precision.HIGHEST
MESH = pl.DeviceIdType.MESH


def mm(a, b):
    return jnp.dot(a, b, preferred_element_type=F32)


def mm_t(a, b):
    return lax.dot_general(a, b, (((1,), (1,)), ((), ())), preferred_element_type=F32)


def sigmoid(x):
    return 0.5 * jnp.tanh(0.5 * x) + 0.5


def iota(shape, dim):
    return lax.broadcasted_iota(jnp.int32, shape, dim)


def kernel(
    n,
    x_ref, ts_ref, lb_ref, mod_ref, win_hbm, ws_ref, conv_ref, sbias_ref, dlog_ref, skip_ref,
    gain_ref, wout_hbm, wq_hbm, wm_hbm, wg_hbm,
    out_ref,
    win, wout, wq, wm, wg, wsem,
    hid, ubuf, gate, ext, act, yloc, gbuf, tri, expand, bias, ones,
    s1, r1, s2, r2, s1s, s1r, s2s, s2r,
    tsend, trecv, tss, tsr, asend, arecv, ass, asr,
    qb, kv, kvp, oacc, mstat, lstat,
):
    rows, width = x_ref.shape
    spans = rows // SPAN
    tok = rows // WINDOW
    part = r2.shape[2]
    me = lax.axis_index("frames")
    nxt = lax.rem(me + 1, n)
    ts = ts_ref[0]

    def weight_copy(layer, k):
        src, dst = ((win_hbm, win), (wout_hbm, wout), (wq_hbm, wq), (wm_hbm, wm), (wg_hbm, wg))[k]
        return pltpu.make_async_copy(src.at[layer], dst.at[layer], wsem.at[layer, k])

    for layer in range(LAYERS):
        for k in range(5):
            weight_copy(layer, k).start()

    barrier = pltpu.get_barrier_semaphore()

    def greet(k, c):
        pl.semaphore_signal(
            barrier, inc=1, device_id={"frames": lax.rem(me + k, n)}, device_id_type=MESH
        )
        return c

    lax.fori_loop(1, n, greet, 0)

    out_ref[...] = x_ref[...].astype(F32)
    tri[...] = jnp.where(iota((SPAN, SPAN), 0) >= iota((SPAN, SPAN), 1), 1.0, 0.0).astype(F32)
    lane_k = iota((LANES, INNER), 0)
    lane_j = iota((LANES, INNER), 1)
    expand[...] = jnp.where(
        (lane_k < 3 * HEADS) & (lax.rem(lane_k, HEADS) == lane_j // HEAD_DIM), 1.0, 0.0
    ).astype(BF16)
    half_a = iota((LANES, LANES), 0) // HEAD_DIM
    half_b = iota((LANES, LANES), 1) // HEAD_DIM
    ones[...] = jnp.where(half_a == half_b, 1.0, 0.0).astype(BF16)
    key_col = iota((tok, rows), 1) // tok
    for f in range(WINDOW):
        reach = lb_ref[f]
        own = (key_col <= f) & (key_col >= f - reach)
        prev = (key_col - WINDOW >= f - reach) & (me > 0)
        bias[f * tok : (f + 1) * tok, 0:rows] = jnp.where(own, 0.0, -1e30)
        bias[f * tok : (f + 1) * tok, rows : 2 * rows] = jnp.where(prev, 0.0, -1e30)
    spread = jnp.where(
        iota((HEADS, LANES), 0) == lax.rem(iota((HEADS, LANES), 1), HEADS), 1.0, 0.0
    ).astype(F32)

    def widen(x):
        group = iota(x.shape, 1) // HEADS
        hi = x.astype(BF16).astype(F32)
        rest = x - hi
        mid = rest.astype(BF16).astype(F32)
        low = rest - mid
        packed = jnp.where(group == 0, hi, jnp.where(group == 1, mid, jnp.where(group == 2, low, 0.0)))
        return packed.astype(BF16)

    def repeat_heads(row):
        return jnp.dot(row, spread, precision=HIGH, preferred_element_type=F32)

    def modulate(src, dst, shift, scale):
        for c in range(spans):
            v = src[c * SPAN : (c + 1) * SPAN, :]
            inv = lax.rsqrt(jnp.mean(v * v, axis=-1, keepdims=True) + EPS)
            dst[c * SPAN : (c + 1) * SPAN, :] = ((v * inv) * (1.0 + scale) + shift).astype(BF16)

    def tail_copy(layer):
        return pltpu.make_async_remote_copy(
            src_ref=tsend.at[layer], dst_ref=trecv.at[layer], send_sem=tss.at[layer],
            recv_sem=tsr.at[layer], device_id={"frames": nxt}, device_id_type=MESH,
        )

    def rows_copy(layer):
        return pltpu.make_async_remote_copy(
            src_ref=asend.at[layer], dst_ref=arecv.at[layer], send_sem=ass.at[layer],
            recv_sem=asr.at[layer], device_id={"frames": nxt}, device_id_type=MESH,
        )

    def gather_copy(layer, to, slot):
        return pltpu.make_async_remote_copy(
            src_ref=s1.at[layer, to], dst_ref=r1.at[layer, slot], send_sem=s1s.at[layer, to],
            recv_sem=s1r.at[layer, slot], device_id={"frames": to}, device_id_type=MESH,
        )

    def return_copy(layer, to, slot):
        return pltpu.make_async_remote_copy(
            src_ref=s2.at[layer, to], dst_ref=r2.at[layer, slot], send_sem=s2s.at[layer, to],
            recv_sem=s2r.at[layer, slot], device_id={"frames": to}, device_id_type=MESH,
        )

    def each_peer(fn):
        def step(k, c):
            fn(lax.rem(me + k, n))
            return c

        lax.fori_loop(1, n, step, 0)

    pl.semaphore_wait(barrier, n - 1)

    first = iota((SPAN, LANES), 1) < HEAD_DIM

    def block(layer, carry):
        mods = mod_ref[layer, ts].astype(F32)
        modulate(out_ref, ubuf, mods[0:1, :], mods[1:2, :])
        weight_copy(layer, 0).wait()
        u = ubuf[...]
        mixed_cols = INNER + 2 * STATE
        for c in range(0, mixed_cols, 256):
            res = mm(u, win[layer, :, INNER + c : INNER + c + 256]).astype(BF16)
            ext[8 : 8 + rows, c : c + 256] = res.astype(F32)
            tsend[layer, :, c : c + 256] = res[rows - 16 :, :]
        tail_copy(layer).start()
        wstep = mm(ws_ref[layer], spread.astype(BF16)).astype(BF16)
        raw = mm(u, wstep) + repeat_heads(sbias_ref[layer, pl.ds(ts, 1), :])
        step = jnp.maximum(raw, 0.0) + jnp.log1p(jnp.exp(-jnp.abs(raw)))
        logd = -jnp.exp(repeat_heads(dlog_ref[pl.ds(layer, 1), :])) * step
        cums = [
            jnp.dot(tri[...], logd[c * SPAN : (c + 1) * SPAN, :], precision=HIGH, preferred_element_type=F32)
            for c in range(spans)
        ]
        steps = [step[c * SPAN : (c + 1) * SPAN, :] for c in range(spans)]
        tail_copy(layer).wait_recv()
        for c in range(0, mixed_cols, 256):
            got = trecv[layer, :, c : c + 256].astype(F32)
            ext[0:8, c : c + 256] = jnp.where(me > 0, got[8:16, :], 0.0)
        taps = conv_ref[layer]
        for c in reversed(range(0, mixed_cols, LANES)):
            for r in range(spans):
                base = 8 - (CONV - 1) + r * SPAN
                total = taps[0:1, c : c + LANES] * ext[base : base + SPAN, c : c + LANES]
                for k in range(1, CONV):
                    total = total + taps[k : k + 1, c : c + LANES] * ext[
                        base + k : base + k + SPAN, c : c + LANES
                    ]
                act[r * SPAN : (r + 1) * SPAN, c : c + LANES] = (total * sigmoid(total)).astype(BF16)
        ends = [cum[SPAN - 1 : SPAN, :] for cum in cums]
        in_map = [act[c * SPAN : (c + 1) * SPAN, INNER : INNER + STATE] for c in range(spans)]
        out_map = [act[c * SPAN : (c + 1) * SPAN, INNER + STATE :] for c in range(spans)]
        in_t = [m.astype(F32).T.astype(BF16) for m in in_map]
        edges = [widen(jnp.exp(ends[c] - cums[c]) * steps[c]) for c in range(spans)]
        end_rows = [widen(jnp.broadcast_to(jnp.exp(e), (16, LANES))) for e in ends]
        befores = []
        for p in range(PAIRS):
            cols = slice(p * LANES, (p + 1) * LANES)
            state = None
            decay = None
            for c in range(spans):
                scaled = act[c * SPAN : (c + 1) * SPAN, cols].astype(F32) * mm(edges[c], expand[:, cols])
                term = mm(in_t[c], scaled.astype(BF16))
                row = mm(end_rows[c], expand[:, cols])
                if state is None:
                    state, decay = term, row
                else:
                    yloc[c * SPAN : (c + 1) * SPAN, cols] = mm(out_map[c], state.astype(BF16))
                    state = row[0:1, :] * state + term
                    decay = row * decay
            per = n // PAIRS
            for k in range(per):
                s1[layer, p * per + k, 0:part, :] = state[k * part : (k + 1) * part, :].astype(BF16)
                s1[layer, p * per + k, part:, :] = decay.astype(BF16)
        each_peer(lambda to: gather_copy(layer, to, me).start())
        r1[layer, me] = s1[layer, me]

        for c in range(0, INNER, 256):
            gate[:, c : c + 256] = mm(u, win[layer, :, c : c + 256]).astype(BF16)
        lower = iota((SPAN, SPAN), 0) >= iota((SPAN, SPAN), 1)
        grow = [None] * spans
        reach_end = None
        for c in range(spans):
            span = slice(c * SPAN, (c + 1) * SPAN)
            cum, cum_t, step_t = cums[c], cums[c].T, steps[c].T
            affinity = jnp.where(lower, mm_t(out_map[c], in_map[c]), 0.0)
            inner_grow = widen(jnp.exp(cum))
            total_log = cum if reach_end is None else cum + reach_end
            grow[c] = widen(jnp.exp(total_log))
            reach_end = ends[c] if reach_end is None else reach_end + ends[c]
            for p in range(PAIRS):
                cols = slice(p * LANES, (p + 1) * LANES)
                values = act[span, cols]
                outs = []
                for h in (2 * p, 2 * p + 1):
                    gaps = jnp.minimum(cum[:, h : h + 1] - cum_t[h : h + 1, :], 0.0)
                    mixing = (affinity * jnp.exp(gaps) * step_t[h : h + 1, :]).astype(BF16)
                    outs.append(mm(mixing, values))
                y = jnp.where(first, outs[0], outs[1])
                if c > 0:
                    y = y + yloc[span, cols] * mm(inner_grow, expand[:, cols])
                yloc[span, cols] = y

        each_peer(lambda frm: gather_copy(layer, frm, frm).wait_recv())
        run = jnp.zeros((part, LANES), F32)
        for k in range(n):
            s2[layer, k] = run.astype(BF16)
            run = r1[layer, k, part : part + 1, :].astype(F32) * run + r1[layer, k, 0:part, :].astype(F32)
        each_peer(lambda to: return_copy(layer, to, me).start())
        r2[layer, me] = s2[layer, me]
        skip_row = widen(repeat_heads(jnp.broadcast_to(skip_ref[pl.ds(layer, 1), :], (16, HEADS))))
        for p in range(PAIRS):
            cols = slice(p * LANES, (p + 1) * LANES)
            skip = mm(skip_row, expand[:, cols])[0:1, :]
            yloc[:, cols] = yloc[:, cols] + skip * act[:, cols].astype(F32)
        each_peer(lambda frm: return_copy(layer, frm, frm).wait_recv())

        gain = gain_ref[pl.ds(layer, 1), :]
        per = n // PAIRS
        for p in range(PAIRS):
            cols = slice(p * LANES, (p + 1) * LANES)
            incoming = r2[layer, p * per : (p + 1) * per].reshape(STATE, LANES)
            for c in range(spans):
                span = slice(c * SPAN, (c + 1) * SPAN)
                carried = mm(out_map[c], incoming) * mm(grow[c], expand[:, cols])
                y = yloc[span, cols] + carried
                z = gate[span, cols].astype(F32)
                g = y * (z * sigmoid(z))
                sq = g * g
                hi = sq.astype(BF16)
                lo = (sq - hi.astype(F32)).astype(BF16)
                ms = (mm(hi, ones[...]) + mm(lo, ones[...])) * (1.0 / HEAD_DIM)
                gbuf[span, cols] = (g * lax.rsqrt(ms + HEAD_EPS) * gain[:, cols]).astype(BF16)
        weight_copy(layer, 1).wait()
        g_all = gbuf[...]
        for c in range(0, width, 256):
            hid[:, c : c + 256] = out_ref[:, c : c + 256] + mm(g_all, wout[layer, :, c : c + 256])
        modulate(hid, asend.at[layer], mods[2:3, :], mods[3:4, :])
        rows_copy(layer).start()
        weight_copy(layer, 2).wait()
        weight_copy(layer, 3).wait()
        a = asend[layer]
        for c in range(0, ATTN, 256):
            q = mm(a, wq[layer, :, c : c + 256]).astype(BF16)
            qb[:, c : c + 256] = (q.astype(F32) * HEAD_DIM ** (-0.5)).astype(BF16)
        for c in range(0, 2 * ATTN, 256):
            kv[:, c : c + 256] = mm(a, wm[layer, :, c : c + 256]).astype(BF16)

        def attend_half(p, h, span, keys, cols, shift):
            q = qb[span, cols]
            mine = first if h == 0 else ~first
            q = jnp.where(mine, q, jnp.zeros_like(q))
            s = mm_t(q, keys[:, cols]) + bias[span, shift : shift + rows]
            top = jnp.max(s, axis=-1, keepdims=True)
            w = jnp.exp(s - top)
            total = jnp.sum(w, axis=-1, keepdims=True)
            vals = keys[:, ATTN + p * LANES : ATTN + (p + 1) * LANES]
            return top, total, mm(w.astype(BF16), vals)

        for p in range(ATTN // LANES):
            cols = slice(p * LANES, (p + 1) * LANES)
            for c in range(spans):
                span = slice(c * SPAN, (c + 1) * SPAN)
                o = []
                for h in range(2):
                    top, total, mixed = attend_half(p, h, span, kv, cols, 0)
                    idx = 2 * p + h
                    mstat[span, idx : idx + 1] = top
                    lstat[span, idx : idx + 1] = total
                    o.append(mixed)
                oacc[span, cols] = jnp.where(first, o[0], o[1])
        rows_copy(layer).wait_recv()
        a = arecv[layer]
        for c in range(0, 2 * ATTN, 256):
            kvp[:, c : c + 256] = mm(a, wm[layer, :, c : c + 256]).astype(BF16)
        for p in range(ATTN // LANES):
            cols = slice(p * LANES, (p + 1) * LANES)
            for c in range(spans):
                span = slice(c * SPAN, (c + 1) * SPAN)
                o, fa, fb = [], [], []
                for h in range(2):
                    top, total, mixed = attend_half(p, h, span, kvp, cols, rows)
                    idx = 2 * p + h
                    top0, total0 = mstat[span, idx : idx + 1], lstat[span, idx : idx + 1]
                    most = jnp.maximum(top, top0)
                    wa, wb = jnp.exp(top0 - most), jnp.exp(top - most)
                    inv = 1.0 / (wa * total0 + wb * total)
                    o.append(mixed)
                    fa.append(wa * inv)
                    fb.append(wb * inv)
                res = oacc[span, cols] * jnp.where(first, fa[0], fa[1]) + jnp.where(
                    first, o[0] * fb[0], o[1] * fb[1]
                )
                gbuf[span, cols] = res.astype(BF16)
        weight_copy(layer, 4).wait()
        att = gbuf[:, 0:ATTN]
        for c in range(0, width, 256):
            out_ref[:, c : c + 256] = hid[:, c : c + 256] + mm(att, wg[layer, :, c : c + 256])
        tail_copy(layer).wait_send()
        rows_copy(layer).wait_send()
        each_peer(lambda to: gather_copy(layer, to, me).wait_send())
        each_peer(lambda to: return_copy(layer, to, me).wait_send())
        return carry

    lax.fori_loop(0, LAYERS, block, 0)


def shards(
    n, latents, timestep, lookback, modulation, input_weight, step_weight, conv_weight, step_bias,
    decay_log, skip_gain, norm_gain, output_weight, query_weight, memory_weight, merge_weight,
):
    frames_dev, tok, width = latents.shape
    rows = frames_dev * tok
    part = INNER * STATE // n // LANES
    vmem = pl.BlockSpec(memory_space=pltpu.VMEM)
    smem = pl.BlockSpec(memory_space=pltpu.SMEM)
    hbm = pl.BlockSpec(memory_space=pl.ANY)
    mixed_cols = INNER + 2 * STATE
    dma = pltpu.SemaphoreType.DMA
    out = pl.pallas_call(
        functools.partial(kernel, n),
        out_shape=jax.ShapeDtypeStruct((rows, width), F32),
        in_specs=[
            vmem, smem, smem, vmem, hbm, vmem, vmem, vmem, vmem, vmem, vmem, hbm, hbm, hbm, hbm,
        ],
        out_specs=vmem,
        scratch_shapes=[
            pltpu.VMEM(input_weight.shape, BF16),
            pltpu.VMEM(output_weight.shape, BF16),
            pltpu.VMEM(query_weight.shape, BF16),
            pltpu.VMEM(memory_weight.shape, BF16),
            pltpu.VMEM(merge_weight.shape, BF16),
            dma((LAYERS, 5)),
            pltpu.VMEM((rows, width), F32),
            pltpu.VMEM((rows, width), BF16),
            pltpu.VMEM((rows, INNER), BF16),
            pltpu.VMEM((rows + 8, mixed_cols), F32),
            pltpu.VMEM((rows, mixed_cols), BF16),
            pltpu.VMEM((rows, INNER), F32),
            pltpu.VMEM((rows, INNER), BF16),
            pltpu.VMEM((SPAN, SPAN), F32),
            pltpu.VMEM((LANES, INNER), BF16),
            pltpu.VMEM((rows, 2 * rows), F32),
            pltpu.VMEM((LANES, LANES), BF16),
            pltpu.VMEM((LAYERS, n, part + 16, LANES), BF16),
            pltpu.VMEM((LAYERS, n, part + 16, LANES), BF16),
            pltpu.VMEM((LAYERS, n, part, LANES), BF16),
            pltpu.VMEM((LAYERS, n, part, LANES), BF16),
            dma((LAYERS, n)), dma((LAYERS, n)), dma((LAYERS, n)), dma((LAYERS, n)),
            pltpu.VMEM((LAYERS, 16, mixed_cols), BF16),
            pltpu.VMEM((LAYERS, 16, mixed_cols), BF16),
            dma((LAYERS,)), dma((LAYERS,)),
            pltpu.VMEM((LAYERS, rows, width), BF16),
            pltpu.VMEM((LAYERS, rows, width), BF16),
            dma((LAYERS,)), dma((LAYERS,)),
            pltpu.VMEM((rows, ATTN), BF16),
            pltpu.VMEM((rows, 2 * ATTN), BF16),
            pltpu.VMEM((rows, 2 * ATTN), BF16),
            pltpu.VMEM((rows, ATTN), F32),
            pltpu.VMEM((rows, LANES), F32),
            pltpu.VMEM((rows, LANES), F32),
        ],
        compiler_params=pltpu.CompilerParams(
            collective_id=0, has_side_effects=True, vmem_limit_bytes=56 * 1024 * 1024
        ),
    )(
        latents.reshape(rows, width), timestep, lookback, modulation, input_weight, step_weight,
        conv_weight, step_bias, decay_log, skip_gain, norm_gain, output_weight, query_weight,
        memory_weight, merge_weight,
    )
    return out.reshape(latents.shape)


def solution(mesh):
    split = P(("groups", "frames"))
    frames = P(("groups", "frames"), None, None)
    return jax.shard_map(
        functools.partial(shards, mesh.shape["frames"]),
        mesh=mesh,
        in_specs=(frames, split, split) + (P(),) * 12,
        out_specs=frames,
        check_vma=False,
    )
```

```python
import functools

import jax
import jax.numpy as jnp
from jax import lax
from jax.experimental import pallas as pl
from jax.experimental.pallas import tpu as pltpu
from jax.sharding import PartitionSpec as P

HEADS = 16
HEAD_DIM = 64
STATE = 128
ATT_HEADS = 8
LAYERS = 2
CONV = 4
SPAN = 128
WINDOW = 8
EPS = 1e-06
HEAD_EPS = 1e-05
LANES = 128
INNER = HEADS * HEAD_DIM
ATTN = ATT_HEADS * HEAD_DIM
PAIRS = INNER // LANES
F32 = jnp.float32
BF16 = jnp.bfloat16
HIGH = lax.Precision.HIGHEST
MESH = pl.DeviceIdType.MESH


def mm(a, b):
    return jnp.dot(a, b, preferred_element_type=F32)


def mm_t(a, b):
    return lax.dot_general(a, b, (((1,), (1,)), ((), ())), preferred_element_type=F32)


def sigmoid(x):
    return 0.5 * jnp.tanh(0.5 * x) + 0.5


def iota(shape, dim):
    return lax.broadcasted_iota(jnp.int32, shape, dim)


def kernel(
    n,
    x_ref, ts_ref, lb_ref, mod_ref, win_hbm, ws_ref, conv_ref, sbias_ref, dlog_ref, skip_ref,
    gain_ref, wout_hbm, wq_hbm, wm_hbm, wg_hbm,
    out_ref,
    win, wout, wq, wm, wg, wsem,
    hid, ubuf, gate, ext, act, yloc, gbuf, tri, expand, bias, ones,
    s1, r1, s2, r2, s1s, s1r, s2s, s2r, cin, cout, cs, cr,
    tsend, trecv, tss, tsr, asend, arecv, ass, asr,
    qb, kv, kvp, oacc, mstat, lstat,
):
    rows, width = x_ref.shape
    spans = rows // SPAN
    tok = rows // WINDOW
    me = lax.axis_index("frames")
    team = PAIRS
    teams = n // team
    mine_team = me // team
    lid = lax.rem(me, team)
    base_id = mine_team * team
    nxt = lax.rem(me + 1, n)
    ts = ts_ref[0]

    def weight_copy(layer, k):
        src, dst = ((win_hbm, win), (wout_hbm, wout), (wq_hbm, wq), (wm_hbm, wm), (wg_hbm, wg))[k]
        return pltpu.make_async_copy(src.at[layer], dst.at[layer], wsem.at[layer, k])

    for layer in range(LAYERS):
        for k in range(5):
            weight_copy(layer, k).start()

    barrier = pltpu.get_barrier_semaphore()

    def greet(k, c):
        pl.semaphore_signal(
            barrier, inc=1, device_id={"frames": lax.rem(me + k, n)}, device_id_type=MESH
        )
        return c

    lax.fori_loop(1, n, greet, 0)

    out_ref[...] = x_ref[...].astype(F32)
    tri[...] = jnp.where(iota((SPAN, SPAN), 0) >= iota((SPAN, SPAN), 1), 1.0, 0.0).astype(F32)
    lane_k = iota((LANES, INNER), 0)
    lane_j = iota((LANES, INNER), 1)
    expand[...] = jnp.where(
        (lane_k < 3 * HEADS) & (lax.rem(lane_k, HEADS) == lane_j // HEAD_DIM), 1.0, 0.0
    ).astype(BF16)
    half_a = iota((LANES, LANES), 0) // HEAD_DIM
    half_b = iota((LANES, LANES), 1) // HEAD_DIM
    ones[...] = jnp.where(half_a == half_b, 1.0, 0.0).astype(BF16)
    key_col = iota((tok, rows), 1) // tok
    for f in range(WINDOW):
        reach = lb_ref[f]
        own = (key_col <= f) & (key_col >= f - reach)
        prev = (key_col - WINDOW >= f - reach) & (me > 0)
        bias[f * tok : (f + 1) * tok, 0:rows] = jnp.where(own, 0.0, -1e30)
        bias[f * tok : (f + 1) * tok, rows : 2 * rows] = jnp.where(prev, 0.0, -1e30)
    spread = jnp.where(
        iota((HEADS, LANES), 0) == lax.rem(iota((HEADS, LANES), 1), HEADS), 1.0, 0.0
    ).astype(F32)

    def widen(x):
        group = iota(x.shape, 1) // HEADS
        hi = x.astype(BF16).astype(F32)
        rest = x - hi
        mid = rest.astype(BF16).astype(F32)
        low = rest - mid
        packed = jnp.where(group == 0, hi, jnp.where(group == 1, mid, jnp.where(group == 2, low, 0.0)))
        return packed.astype(BF16)

    def repeat_heads(row):
        return jnp.dot(row, spread, precision=HIGH, preferred_element_type=F32)

    def modulate(src, dst, shift, scale, which):
        for c in which:
            v = src[c * SPAN : (c + 1) * SPAN, :]
            inv = lax.rsqrt(jnp.mean(v * v, axis=-1, keepdims=True) + EPS)
            dst[c * SPAN : (c + 1) * SPAN, :] = ((v * inv) * (1.0 + scale) + shift).astype(BF16)

    def tail_copy(layer):
        return pltpu.make_async_remote_copy(
            src_ref=tsend.at[layer], dst_ref=trecv.at[layer], send_sem=tss.at[layer],
            recv_sem=tsr.at[layer], device_id={"frames": nxt}, device_id_type=MESH,
        )

    def rows_copy(layer, c):
        span = pl.ds(c * SPAN, SPAN)
        return pltpu.make_async_remote_copy(
            src_ref=asend.at[layer, span], dst_ref=arecv.at[layer, span], send_sem=ass.at[layer, c],
            recv_sem=asr.at[layer, c], device_id={"frames": nxt}, device_id_type=MESH,
        )

    def gather_copy(layer, owner, slot):
        return pltpu.make_async_remote_copy(
            src_ref=s1.at[layer, owner], dst_ref=r1.at[layer, slot], send_sem=s1s.at[layer, owner],
            recv_sem=s1r.at[layer, slot], device_id={"frames": base_id + owner}, device_id_type=MESH,
        )

    def return_copy(layer, to, slot):
        return pltpu.make_async_remote_copy(
            src_ref=s2.at[layer, to], dst_ref=r2.at[layer, slot], send_sem=s2s.at[layer, to],
            recv_sem=s2r.at[layer, slot], device_id={"frames": base_id + to}, device_id_type=MESH,
        )

    def chain_copy(layer):
        return pltpu.make_async_remote_copy(
            src_ref=cout.at[layer], dst_ref=cin.at[layer], send_sem=cs.at[layer],
            recv_sem=cr.at[layer], device_id={"frames": lax.rem(me + team, n)}, device_id_type=MESH,
        )

    def unless_me(k, fn):
        @pl.when(lid != k)
        def _():
            fn()

    @pl.when(mine_team == 0)
    def _():
        cin[...] = jnp.zeros_like(cin)

    first = iota((SPAN, LANES), 1) < HEAD_DIM

    def block(layer, carry):
        mods = mod_ref[layer, ts].astype(F32)
        modulate(out_ref, ubuf, mods[0:1, :], mods[1:2, :], range(spans))
        weight_copy(layer, 0).wait()
        u = ubuf[...]
        mixed_cols = INNER + 2 * STATE
        for c in range(0, mixed_cols, 256):
            res = mm(u, win[layer, :, INNER + c : INNER + c + 256]).astype(BF16)
            ext[8 : 8 + rows, c : c + 256] = res.astype(F32)
            tsend[layer, :, c : c + 256] = res[rows - 16 :, :]

        @pl.when(layer == 0)
        def _():
            pl.semaphore_wait(barrier, n - 1)

        tail_copy(layer).start()
        for c in range(0, INNER, 256):
            gate[:, c : c + 256] = mm(u, win[layer, :, c : c + 256]).astype(BF16)
        wstep = lax.dot_general(
            spread.astype(BF16), ws_ref[layer], (((0,), (0,)), ((), ())), preferred_element_type=F32
        ).astype(BF16)
        sbias = sbias_ref[layer]
        here = jnp.where(iota(sbias.shape, 1) == ts, sbias, 0.0)
        here = jnp.sum(jnp.sum(here, axis=-1, keepdims=True) * spread, axis=0, keepdims=True)
        raw = mm_t(u, wstep) + here
        step = jnp.maximum(raw, 0.0) + jnp.log1p(jnp.exp(-jnp.abs(raw)))
        logd = -jnp.exp(repeat_heads(dlog_ref[pl.ds(layer, 1), :])) * step
        cums = [
            jnp.dot(tri[...], logd[c * SPAN : (c + 1) * SPAN, :], precision=HIGH, preferred_element_type=F32)
            for c in range(spans)
        ]
        steps = [step[c * SPAN : (c + 1) * SPAN, :] for c in range(spans)]
        taps = conv_ref[layer]
        for r in reversed(range(spans)):
            if r == 0:
                tail_copy(layer).wait_recv()
                for c in range(0, mixed_cols, 256):
                    got = trecv[layer, :, c : c + 256].astype(F32)
                    ext[0:8, c : c + 256] = jnp.where(me > 0, got[8:16, :], 0.0)
            base = 8 - (CONV - 1) + r * SPAN
            for c in range(0, mixed_cols, LANES):
                total = taps[0:1, c : c + LANES] * ext[base : base + SPAN, c : c + LANES]
                for k in range(1, CONV):
                    total = total + taps[k : k + 1, c : c + LANES] * ext[
                        base + k : base + k + SPAN, c : c + LANES
                    ]
                act[r * SPAN : (r + 1) * SPAN, c : c + LANES] = (total * sigmoid(total)).astype(BF16)
        ends = [cum[SPAN - 1 : SPAN, :] for cum in cums]
        in_map = [act[c * SPAN : (c + 1) * SPAN, INNER : INNER + STATE] for c in range(spans)]
        out_map = [act[c * SPAN : (c + 1) * SPAN, INNER + STATE :] for c in range(spans)]
        in_t = [m.astype(F32).T.astype(BF16) for m in in_map]
        edges = [widen(jnp.exp(ends[c] - cums[c]) * steps[c]) for c in range(spans)]
        end_rows = [widen(jnp.broadcast_to(jnp.exp(e), (16, LANES))) for e in ends]
        befores = []
        for p in range(PAIRS):
            cols = slice(p * LANES, (p + 1) * LANES)
            state = None
            decay = None
            for c in range(spans):
                scaled = act[c * SPAN : (c + 1) * SPAN, cols].astype(F32) * mm(edges[c], expand[:, cols])
                term = mm(in_t[c], scaled.astype(BF16))
                row = mm(end_rows[c], expand[:, cols])
                if state is None:
                    state, decay = term, row
                else:
                    yloc[c * SPAN : (c + 1) * SPAN, cols] = mm(out_map[c], state.astype(BF16))
                    state = row[0:1, :] * state + term
                    decay = row * decay
            s1[layer, p, 0:STATE, :] = state.astype(BF16)
            s1[layer, p, STATE:, :] = decay.astype(BF16)
            unless_me(p, lambda: gather_copy(layer, p, lid).start())
        r1[layer, lid] = s1[layer, lid]

        lower = iota((SPAN, SPAN), 0) >= iota((SPAN, SPAN), 1)
        grow = [None] * spans
        reach_end = None
        for c in range(spans):
            span = slice(c * SPAN, (c + 1) * SPAN)
            cum, cum_t, step_t = cums[c], cums[c].T, steps[c].T
            affinity = jnp.where(lower, mm_t(out_map[c], in_map[c]), 0.0)
            inner_grow = widen(jnp.exp(cum))
            total_log = cum if reach_end is None else cum + reach_end
            grow[c] = widen(jnp.exp(total_log))
            reach_end = ends[c] if reach_end is None else reach_end + ends[c]
            for p in range(PAIRS):
                cols = slice(p * LANES, (p + 1) * LANES)
                values = act[span, cols]
                outs = []
                for h in (2 * p, 2 * p + 1):
                    gaps = jnp.minimum(cum[:, h : h + 1] - cum_t[h : h + 1, :], 0.0)
                    mixing = (affinity * jnp.exp(gaps) * step_t[h : h + 1, :]).astype(BF16)
                    outs.append(mm(mixing, values))
                y = jnp.where(first, outs[0], outs[1])
                if c > 0:
                    y = y + yloc[span, cols] * mm(inner_grow, expand[:, cols])
                yloc[span, cols] = y

        run = jnp.zeros((STATE, LANES), F32)
        whole = jnp.ones((1, LANES), F32)
        for k in range(team):
            unless_me(k, lambda: gather_copy(layer, k, k).wait_recv())
            decay = r1[layer, k, STATE : STATE + 1, :].astype(F32)
            run = decay * run + r1[layer, k, 0:STATE, :].astype(F32)
            whole = whole * decay

        @pl.when(mine_team > 0)
        def _():
            chain_copy(layer).wait_recv()

        before = cin[layer].astype(F32)
        cout[layer] = (whole * before + run).astype(BF16)

        @pl.when(mine_team < teams - 1)
        def _():
            chain_copy(layer).start()

        for k in range(team):
            s2[layer, k] = before.astype(BF16)
            unless_me(k, lambda: return_copy(layer, k, lid).start())
            before = r1[layer, k, STATE : STATE + 1, :].astype(F32) * before + r1[
                layer, k, 0:STATE, :
            ].astype(F32)
        r2[layer, lid] = s2[layer, lid]
        skip_row = widen(repeat_heads(jnp.broadcast_to(skip_ref[pl.ds(layer, 1), :], (16, HEADS))))
        for p in range(PAIRS):
            cols = slice(p * LANES, (p + 1) * LANES)
            skip = mm(skip_row, expand[:, cols])[0:1, :]
            yloc[:, cols] = yloc[:, cols] + skip * act[:, cols].astype(F32)

        gain = gain_ref[pl.ds(layer, 1), :]
        for p in range(PAIRS):
            cols = slice(p * LANES, (p + 1) * LANES)
            unless_me(p, lambda: return_copy(layer, p, p).wait_recv())
            incoming = r2[layer, p]
            for c in range(spans):
                span = slice(c * SPAN, (c + 1) * SPAN)
                carried = mm(out_map[c], incoming) * mm(grow[c], expand[:, cols])
                y = yloc[span, cols] + carried
                z = gate[span, cols].astype(F32)
                g = y * (z * sigmoid(z))
                sq = g * g
                hi = sq.astype(BF16)
                lo = (sq - hi.astype(F32)).astype(BF16)
                ms = (mm(hi, ones[...]) + mm(lo, ones[...])) * (1.0 / HEAD_DIM)
                gbuf[span, cols] = (g * lax.rsqrt(ms + HEAD_EPS) * gain[:, cols]).astype(BF16)
        weight_copy(layer, 1).wait()
        for r in range(spans):
            span = slice(r * SPAN, (r + 1) * SPAN)
            for c in range(0, width, 256):
                hid[span, c : c + 256] = out_ref[span, c : c + 256] + mm(
                    gbuf[span, :], wout[layer, :, c : c + 256]
                )
            modulate(hid, asend.at[layer], mods[2:3, :], mods[3:4, :], [r])
            rows_copy(layer, r).start()
        weight_copy(layer, 2).wait()
        weight_copy(layer, 3).wait()
        a = asend[layer]
        for c in range(0, ATTN, 256):
            q = mm(a, wq[layer, :, c : c + 256]).astype(BF16)
            qb[:, c : c + 256] = (q.astype(F32) * HEAD_DIM ** (-0.5)).astype(BF16)
        for c in range(0, 2 * ATTN, 256):
            kv[:, c : c + 256] = mm(a, wm[layer, :, c : c + 256]).astype(BF16)

        def attend(p, span, keys, lo, hi, shift):
            cols = slice(p * LANES, (p + 1) * LANES)
            q, k = qb[span, cols], keys[lo:hi, cols]
            vals = keys[lo:hi, ATTN + p * LANES : ATTN + (p + 1) * LANES]
            lanes = iota(vals.shape, 1) < HEAD_DIM
            tops, mixes = [], []
            for h in range(2):
                mine = first if h == 0 else ~first
                s = mm_t(jnp.where(mine, q, jnp.zeros_like(q)), k) + bias[span, shift + lo : shift + hi]
                top = jnp.max(s, axis=-1, keepdims=True)
                mine = lanes if h == 0 else ~lanes
                w = jnp.exp(s - top).astype(BF16)
                mixes.append(mm(w, jnp.where(mine, vals, jnp.ones_like(vals))))
                tops.append(top)
            top = jnp.where(first, tops[0], tops[1])
            total = pltpu.roll(jnp.where(first, mixes[1], mixes[0]), HEAD_DIM, 1)
            return top, total, jnp.where(first, mixes[0], mixes[1])

        for p in range(ATTN // LANES):
            cols = slice(p * LANES, (p + 1) * LANES)
            for c in range(spans):
                span = slice(c * SPAN, (c + 1) * SPAN)
                top, total, mixed = attend(p, span, kv, 0, (c + 1) * SPAN, 0)
                mstat[span, cols] = top
                lstat[span, cols] = total
                oacc[span, cols] = mixed
        for c in range(spans):
            rows_copy(layer, c).wait_recv()
        a = arecv[layer]
        for c in range(0, 2 * ATTN, 256):
            kvp[:, c : c + 256] = mm(a, wm[layer, :, c : c + 256]).astype(BF16)
        for p in range(ATTN // LANES):
            cols = slice(p * LANES, (p + 1) * LANES)
            for c in range(spans):
                span = slice(c * SPAN, (c + 1) * SPAN)
                top, total, mixed = attend(p, span, kvp, c * SPAN, rows, rows)
                top0 = mstat[span, cols]
                most = jnp.maximum(top, top0)
                wa, wb = jnp.exp(top0 - most), jnp.exp(top - most)
                inv = 1.0 / (wa * lstat[span, cols] + wb * total)
                gbuf[span, cols] = ((wa * oacc[span, cols] + wb * mixed) * inv).astype(BF16)
        weight_copy(layer, 4).wait()
        att = gbuf[:, 0:ATTN]
        for c in range(0, width, 256):
            out_ref[:, c : c + 256] = hid[:, c : c + 256] + mm(att, wg[layer, :, c : c + 256])
        tail_copy(layer).wait_send()
        for c in range(spans):
            rows_copy(layer, c).wait_send()
        for k in range(team):
            unless_me(k, lambda: gather_copy(layer, k, lid).wait_send())
            unless_me(k, lambda: return_copy(layer, k, lid).wait_send())

        @pl.when(mine_team < teams - 1)
        def _():
            chain_copy(layer).wait_send()

        return carry

    lax.fori_loop(0, LAYERS, block, 0)


def shards(
    n, latents, timestep, lookback, modulation, input_weight, step_weight, conv_weight, step_bias,
    decay_log, skip_gain, norm_gain, output_weight, query_weight, memory_weight, merge_weight,
):
    frames_dev, tok, width = latents.shape
    rows = frames_dev * tok
    assert n % PAIRS == 0
    vmem = pl.BlockSpec(memory_space=pltpu.VMEM)
    smem = pl.BlockSpec(memory_space=pltpu.SMEM)
    hbm = pl.BlockSpec(memory_space=pl.ANY)
    mixed_cols = INNER + 2 * STATE
    dma = pltpu.SemaphoreType.DMA
    out = pl.pallas_call(
        functools.partial(kernel, n),
        out_shape=jax.ShapeDtypeStruct((rows, width), F32),
        in_specs=[
            vmem, smem, smem, vmem, hbm, vmem, vmem, vmem, vmem, vmem, vmem, hbm, hbm, hbm, hbm,
        ],
        out_specs=vmem,
        scratch_shapes=[
            pltpu.VMEM(input_weight.shape, BF16),
            pltpu.VMEM(output_weight.shape, BF16),
            pltpu.VMEM(query_weight.shape, BF16),
            pltpu.VMEM(memory_weight.shape, BF16),
            pltpu.VMEM(merge_weight.shape, BF16),
            dma((LAYERS, 5)),
            pltpu.VMEM((rows, width), F32),
            pltpu.VMEM((rows, width), BF16),
            pltpu.VMEM((rows, INNER), BF16),
            pltpu.VMEM((rows + 8, mixed_cols), F32),
            pltpu.VMEM((rows, mixed_cols), BF16),
            pltpu.VMEM((rows, INNER), F32),
            pltpu.VMEM((rows, INNER), BF16),
            pltpu.VMEM((SPAN, SPAN), F32),
            pltpu.VMEM((LANES, INNER), BF16),
            pltpu.VMEM((rows, 2 * rows), F32),
            pltpu.VMEM((LANES, LANES), BF16),
            pltpu.VMEM((LAYERS, PAIRS, STATE + 16, LANES), BF16),
            pltpu.VMEM((LAYERS, PAIRS, STATE + 16, LANES), BF16),
            pltpu.VMEM((LAYERS, PAIRS, STATE, LANES), BF16),
            pltpu.VMEM((LAYERS, PAIRS, STATE, LANES), BF16),
            dma((LAYERS, PAIRS)), dma((LAYERS, PAIRS)), dma((LAYERS, PAIRS)), dma((LAYERS, PAIRS)),
            pltpu.VMEM((LAYERS, STATE, LANES), BF16),
            pltpu.VMEM((LAYERS, STATE, LANES), BF16),
            dma((LAYERS,)), dma((LAYERS,)),
            pltpu.VMEM((LAYERS, 16, mixed_cols), BF16),
            pltpu.VMEM((LAYERS, 16, mixed_cols), BF16),
            dma((LAYERS,)), dma((LAYERS,)),
            pltpu.VMEM((LAYERS, rows, width), BF16),
            pltpu.VMEM((LAYERS, rows, width), BF16),
            dma((LAYERS, rows // SPAN)), dma((LAYERS, rows // SPAN)),
            pltpu.VMEM((rows, ATTN), BF16),
            pltpu.VMEM((rows, 2 * ATTN), BF16),
            pltpu.VMEM((rows, 2 * ATTN), BF16),
            pltpu.VMEM((rows, ATTN), F32),
            pltpu.VMEM((rows, ATTN), F32),
            pltpu.VMEM((rows, ATTN), F32),
        ],
        compiler_params=pltpu.CompilerParams(
            collective_id=0, has_side_effects=True, vmem_limit_bytes=56 * 1024 * 1024
        ),
    )(
        latents.reshape(rows, width), timestep, lookback, modulation, input_weight,
        jnp.swapaxes(step_weight, 1, 2), conv_weight, jnp.swapaxes(step_bias, 1, 2), decay_log, skip_gain, norm_gain, output_weight, query_weight,
        memory_weight, merge_weight,
    )
    return out.reshape(latents.shape)


def solution(mesh):
    split = P(("groups", "frames"))
    frames = P(("groups", "frames"), None, None)
    return jax.shard_map(
        functools.partial(shards, mesh.shape["frames"]),
        mesh=mesh,
        in_specs=(frames, split, split) + (P(),) * 12,
        out_specs=frames,
        check_vma=False,
    )
```

```python
import functools

import jax
import jax.numpy as jnp
from jax import lax
from jax.experimental import pallas as pl
from jax.experimental.pallas import tpu as pltpu
from jax.sharding import PartitionSpec as P

HEADS = 16
HEAD_DIM = 64
STATE = 128
ATT_HEADS = 8
LAYERS = 2
CONV = 4
SPAN = 128
WINDOW = 8
EPS = 1e-06
HEAD_EPS = 1e-05
LANES = 128
INNER = HEADS * HEAD_DIM
ATTN = ATT_HEADS * HEAD_DIM
PAIRS = INNER // LANES
F32 = jnp.float32
BF16 = jnp.bfloat16
HIGH = lax.Precision.HIGHEST
MESH = pl.DeviceIdType.MESH


def mm(a, b):
    return jnp.dot(a, b, preferred_element_type=F32)


def mm_t(a, b):
    return lax.dot_general(a, b, (((1,), (1,)), ((), ())), preferred_element_type=F32)


def sigmoid(x):
    return 0.5 * jnp.tanh(0.5 * x) + 0.5


def iota(shape, dim):
    return lax.broadcasted_iota(jnp.int32, shape, dim)


def kernel(
    n,
    x_ref, ts_ref, lb_ref, mod_ref, win_hbm, ws_ref, conv_ref, sbias_ref, dlog_ref, skip_ref,
    gain_ref, wout_hbm, wq_hbm, wm_hbm, wg_hbm,
    out_ref,
    win, wout, wq, wm, wg, wsem,
    hid, ubuf, gate, ext, act, yloc, gbuf, tri, expand, bias, ones,
    s1, r1, s2, r2, s1s, s1r, s2s, s2r, cin, cout, cs, cr,
    tsend, trecv, tss, tsr, asend, arecv, ass, asr,
    qb, kv, kvp, oacc, mstat, lstat, swish, growx,
):
    rows, width = x_ref.shape
    spans = rows // SPAN
    tok = rows // WINDOW
    me = lax.axis_index("frames")
    team = PAIRS
    teams = n // team
    mine_team = me // team
    lid = lax.rem(me, team)
    base_id = mine_team * team
    nxt = lax.rem(me + 1, n)
    ts = ts_ref[0]

    def weight_copy(layer, k):
        src, dst = ((win_hbm, win), (wout_hbm, wout), (wq_hbm, wq), (wm_hbm, wm), (wg_hbm, wg))[k]
        return pltpu.make_async_copy(src.at[layer], dst.at[layer], wsem.at[layer, k])

    for layer in range(LAYERS):
        for k in range(5):
            weight_copy(layer, k).start()

    barrier = pltpu.get_barrier_semaphore()

    def greet(k, c):
        pl.semaphore_signal(
            barrier, inc=1, device_id={"frames": lax.rem(me + k, n)}, device_id_type=MESH
        )
        return c

    lax.fori_loop(1, n, greet, 0)

    out_ref[...] = x_ref[...].astype(F32)
    tri[...] = jnp.where(iota((SPAN, SPAN), 0) >= iota((SPAN, SPAN), 1), 1.0, 0.0).astype(F32)
    lane_k = iota((LANES, INNER), 0)
    lane_j = iota((LANES, INNER), 1)
    expand[...] = jnp.where(
        (lane_k < 3 * HEADS) & (lax.rem(lane_k, HEADS) == lane_j // HEAD_DIM), 1.0, 0.0
    ).astype(BF16)
    half_a = iota((LANES, LANES), 0) // HEAD_DIM
    half_b = iota((LANES, LANES), 1) // HEAD_DIM
    ones[...] = jnp.where(half_a == half_b, 1.0, 0.0).astype(BF16)
    key_col = iota((tok, rows), 1) // tok
    for f in range(WINDOW):
        reach = lb_ref[f]
        own = (key_col <= f) & (key_col >= f - reach)
        prev = (key_col - WINDOW >= f - reach) & (me > 0)
        bias[f * tok : (f + 1) * tok, 0:rows] = jnp.where(own, 0.0, -1e30)
        bias[f * tok : (f + 1) * tok, rows : 2 * rows] = jnp.where(prev, 0.0, -1e30)
    spread = jnp.where(
        iota((HEADS, LANES), 0) == lax.rem(iota((HEADS, LANES), 1), HEADS), 1.0, 0.0
    ).astype(F32)

    def widen(x):
        group = iota(x.shape, 1) // HEADS
        hi = x.astype(BF16).astype(F32)
        rest = x - hi
        mid = rest.astype(BF16).astype(F32)
        low = rest - mid
        packed = jnp.where(group == 0, hi, jnp.where(group == 1, mid, jnp.where(group == 2, low, 0.0)))
        return packed.astype(BF16)

    def repeat_heads(row):
        return jnp.dot(row, spread, precision=HIGH, preferred_element_type=F32)

    def modulate(src, dst, shift, scale, which):
        for c in which:
            v = src[c * SPAN : (c + 1) * SPAN, :]
            inv = lax.rsqrt(jnp.mean(v * v, axis=-1, keepdims=True) + EPS)
            dst[c * SPAN : (c + 1) * SPAN, :] = ((v * inv) * (1.0 + scale) + shift).astype(BF16)

    def tail_copy(layer):
        return pltpu.make_async_remote_copy(
            src_ref=tsend.at[layer], dst_ref=trecv.at[layer], send_sem=tss.at[layer],
            recv_sem=tsr.at[layer], device_id={"frames": nxt}, device_id_type=MESH,
        )

    def rows_copy(layer, c):
        span = pl.ds(c * SPAN, SPAN)
        return pltpu.make_async_remote_copy(
            src_ref=asend.at[layer, span], dst_ref=arecv.at[layer, span], send_sem=ass.at[layer, c],
            recv_sem=asr.at[layer, c], device_id={"frames": nxt}, device_id_type=MESH,
        )

    def gather_copy(layer, owner, slot):
        return pltpu.make_async_remote_copy(
            src_ref=s1.at[layer, owner], dst_ref=r1.at[layer, slot], send_sem=s1s.at[layer, owner],
            recv_sem=s1r.at[layer, slot], device_id={"frames": base_id + owner}, device_id_type=MESH,
        )

    def return_copy(layer, to, slot):
        return pltpu.make_async_remote_copy(
            src_ref=s2.at[layer, to], dst_ref=r2.at[layer, slot], send_sem=s2s.at[layer, to],
            recv_sem=s2r.at[layer, slot], device_id={"frames": base_id + to}, device_id_type=MESH,
        )

    def chain_copy(layer):
        return pltpu.make_async_remote_copy(
            src_ref=cout.at[layer], dst_ref=cin.at[layer], send_sem=cs.at[layer],
            recv_sem=cr.at[layer], device_id={"frames": lax.rem(me + team, n)}, device_id_type=MESH,
        )

    def each_mate(fn):
        def step(k, c):
            fn(lax.rem(lid + k, team))
            return c

        lax.fori_loop(1, team, step, 0)

    def unless_me(k, fn):
        @pl.when(lid != k)
        def _():
            fn()

    @pl.when(mine_team == 0)
    def _():
        cin[...] = jnp.zeros_like(cin)

    first = iota((SPAN, LANES), 1) < HEAD_DIM

    def block(layer, carry):
        mods = mod_ref[layer, ts].astype(F32)
        modulate(out_ref, ubuf, mods[0:1, :], mods[1:2, :], range(spans))
        weight_copy(layer, 0).wait()
        u = ubuf[...]
        mixed_cols = INNER + 2 * STATE
        for c in range(0, mixed_cols, 256):
            res = mm(u, win[layer, :, INNER + c : INNER + c + 256]).astype(BF16)
            ext[8 : 8 + rows, c : c + 256] = res.astype(F32)
            tsend[layer, :, c : c + 256] = res[rows - 16 :, :]

        @pl.when(layer == 0)
        def _():
            pl.semaphore_wait(barrier, n - 1)

        tail_copy(layer).start()
        for c in range(0, INNER, 256):
            gate[:, c : c + 256] = mm(u, win[layer, :, c : c + 256]).astype(BF16)
        wstep = lax.dot_general(
            spread.astype(BF16), ws_ref[layer], (((0,), (0,)), ((), ())), preferred_element_type=F32
        ).astype(BF16)
        sbias = sbias_ref[layer]
        here = jnp.where(iota(sbias.shape, 1) == ts, sbias, 0.0)
        here = jnp.sum(jnp.sum(here, axis=-1, keepdims=True) * spread, axis=0, keepdims=True)
        raw = mm_t(u, wstep) + here
        step = jnp.maximum(raw, 0.0) + jnp.log1p(jnp.exp(-jnp.abs(raw)))
        logd = -jnp.exp(repeat_heads(dlog_ref[pl.ds(layer, 1), :])) * step
        cums = [
            jnp.dot(tri[...], logd[c * SPAN : (c + 1) * SPAN, :], precision=HIGH, preferred_element_type=F32)
            for c in range(spans)
        ]
        steps = [step[c * SPAN : (c + 1) * SPAN, :] for c in range(spans)]
        taps = conv_ref[layer]
        for r in reversed(range(spans)):
            if r == 0:
                tail_copy(layer).wait_recv()
                for c in range(0, mixed_cols, 256):
                    got = trecv[layer, :, c : c + 256].astype(F32)
                    ext[0:8, c : c + 256] = jnp.where(me > 0, got[8:16, :], 0.0)
            base = 8 - (CONV - 1) + r * SPAN
            for c in range(0, mixed_cols, LANES):
                total = taps[0:1, c : c + LANES] * ext[base : base + SPAN, c : c + LANES]
                for k in range(1, CONV):
                    total = total + taps[k : k + 1, c : c + LANES] * ext[
                        base + k : base + k + SPAN, c : c + LANES
                    ]
                act[r * SPAN : (r + 1) * SPAN, c : c + LANES] = (total * sigmoid(total)).astype(BF16)
        ends = [cum[SPAN - 1 : SPAN, :] for cum in cums]
        in_map = [act[c * SPAN : (c + 1) * SPAN, INNER : INNER + STATE] for c in range(spans)]
        out_map = [act[c * SPAN : (c + 1) * SPAN, INNER + STATE :] for c in range(spans)]
        in_t = [m.astype(F32).T.astype(BF16) for m in in_map]
        edges = [widen(jnp.exp(ends[c] - cums[c]) * steps[c]) for c in range(spans)]
        end_rows = [widen(jnp.broadcast_to(jnp.exp(e), (16, LANES))) for e in ends]
        befores = []
        for p in range(PAIRS):
            cols = slice(p * LANES, (p + 1) * LANES)
            state = None
            decay = None
            for c in range(spans):
                scaled = act[c * SPAN : (c + 1) * SPAN, cols].astype(F32) * mm(edges[c], expand[:, cols])
                term = mm(in_t[c], scaled.astype(BF16))
                row = mm(end_rows[c], expand[:, cols])
                if state is None:
                    state, decay = term, row
                else:
                    yloc[c * SPAN : (c + 1) * SPAN, cols] = mm(out_map[c], state.astype(BF16))
                    state = row[0:1, :] * state + term
                    decay = row * decay
            s1[layer, p, 0:STATE, :] = state.astype(BF16)
            s1[layer, p, STATE:, :] = decay.astype(BF16)
        each_mate(lambda to: gather_copy(layer, to, lid).start())
        r1[layer, lid] = s1[layer, lid]

        lower = iota((SPAN, SPAN), 0) >= iota((SPAN, SPAN), 1)
        grow = [None] * spans
        reach_end = None
        for c in range(spans):
            span = slice(c * SPAN, (c + 1) * SPAN)
            cum, cum_t, step_t = cums[c], cums[c].T, steps[c].T
            affinity = jnp.where(lower, mm_t(out_map[c], in_map[c]), 0.0)
            inner_grow = widen(jnp.exp(cum))
            total_log = cum if reach_end is None else cum + reach_end
            grow[c] = widen(jnp.exp(total_log))
            reach_end = ends[c] if reach_end is None else reach_end + ends[c]
            for p in range(PAIRS):
                cols = slice(p * LANES, (p + 1) * LANES)
                values = act[span, cols]
                outs = []
                for h in (2 * p, 2 * p + 1):
                    gaps = jnp.minimum(cum[:, h : h + 1] - cum_t[h : h + 1, :], 0.0)
                    mixing = (affinity * jnp.exp(gaps) * step_t[h : h + 1, :]).astype(BF16)
                    outs.append(mm(mixing, values))
                y = jnp.where(first, outs[0], outs[1])
                if c > 0:
                    y = y + yloc[span, cols] * mm(inner_grow, expand[:, cols])
                yloc[span, cols] = y

        run = jnp.zeros((STATE, LANES), F32)
        whole = jnp.ones((1, LANES), F32)
        for k in range(team):
            unless_me(k, lambda: gather_copy(layer, k, k).wait_recv())
            decay = r1[layer, k, STATE : STATE + 1, :].astype(F32)
            run = decay * run + r1[layer, k, 0:STATE, :].astype(F32)
            whole = whole * decay

        @pl.when(mine_team > 0)
        def _():
            chain_copy(layer).wait_recv()

        before = cin[layer].astype(F32)
        cout[layer] = (whole * before + run).astype(BF16)

        @pl.when(mine_team < teams - 1)
        def _():
            chain_copy(layer).start()

        for k in range(team):
            s2[layer, k] = before.astype(BF16)
            before = r1[layer, k, STATE : STATE + 1, :].astype(F32) * before + r1[
                layer, k, 0:STATE, :
            ].astype(F32)
        each_mate(lambda to: return_copy(layer, to, lid).start())
        r2[layer, lid] = s2[layer, lid]
        skip_row = widen(repeat_heads(jnp.broadcast_to(skip_ref[pl.ds(layer, 1), :], (16, HEADS))))
        for p in range(PAIRS):
            cols = slice(p * LANES, (p + 1) * LANES)
            skip = mm(skip_row, expand[:, cols])[0:1, :]
            for c in range(spans):
                span = slice(c * SPAN, (c + 1) * SPAN)
                yloc[span, cols] = yloc[span, cols] + skip * act[span, cols].astype(F32)
                z = gate[span, cols].astype(F32)
                swish[span, cols] = z * sigmoid(z)
                growx[span, cols] = mm(grow[c], expand[:, cols])

        gain = gain_ref[pl.ds(layer, 1), :]
        for p in range(PAIRS):
            cols = slice(p * LANES, (p + 1) * LANES)
            unless_me(p, lambda: return_copy(layer, p, p).wait_recv())
            incoming = r2[layer, p]
            for c in range(spans):
                span = slice(c * SPAN, (c + 1) * SPAN)
                carried = mm(out_map[c], incoming) * growx[span, cols]
                y = yloc[span, cols] + carried
                g = y * swish[span, cols]
                sq = g * g
                hi = sq.astype(BF16)
                lo = (sq - hi.astype(F32)).astype(BF16)
                ms = (mm(hi, ones[...]) + mm(lo, ones[...])) * (1.0 / HEAD_DIM)
                gbuf[span, cols] = (g * lax.rsqrt(ms + HEAD_EPS) * gain[:, cols]).astype(BF16)
        weight_copy(layer, 1).wait()
        for r in reversed(range(spans)):
            span = slice(r * SPAN, (r + 1) * SPAN)
            for c in range(0, width, 256):
                hid[span, c : c + 256] = out_ref[span, c : c + 256] + mm(
                    gbuf[span, :], wout[layer, :, c : c + 256]
                )
            modulate(hid, asend.at[layer], mods[2:3, :], mods[3:4, :], [r])
            rows_copy(layer, r).start()
        weight_copy(layer, 2).wait()
        weight_copy(layer, 3).wait()
        a = asend[layer]
        for c in range(0, ATTN, 256):
            q = mm(a, wq[layer, :, c : c + 256]).astype(BF16)
            qb[:, c : c + 256] = (q.astype(F32) * HEAD_DIM ** (-0.5)).astype(BF16)
        for c in range(0, 2 * ATTN, 256):
            kv[:, c : c + 256] = mm(a, wm[layer, :, c : c + 256]).astype(BF16)

        def attend(p, span, keys, lo, hi, shift):
            cols = slice(p * LANES, (p + 1) * LANES)
            q, k = qb[span, cols], keys[lo:hi, cols]
            vals = keys[lo:hi, ATTN + p * LANES : ATTN + (p + 1) * LANES]
            lanes = iota(vals.shape, 1) < HEAD_DIM
            tops, mixes = [], []
            for h in range(2):
                mine = first if h == 0 else ~first
                s = mm_t(jnp.where(mine, q, jnp.zeros_like(q)), k) + bias[span, shift + lo : shift + hi]
                top = jnp.max(s, axis=-1, keepdims=True)
                mine = lanes if h == 0 else ~lanes
                w = jnp.exp(s - top).astype(BF16)
                mixes.append(mm(w, jnp.where(mine, vals, jnp.ones_like(vals))))
                tops.append(top)
            top = jnp.where(first, tops[0], tops[1])
            total = pltpu.roll(jnp.where(first, mixes[1], mixes[0]), HEAD_DIM, 1)
            return top, total, jnp.where(first, mixes[0], mixes[1])

        for p in range(ATTN // LANES):
            cols = slice(p * LANES, (p + 1) * LANES)
            for c in range(spans):
                span = slice(c * SPAN, (c + 1) * SPAN)
                top, total, mixed = attend(p, span, kv, 0, (c + 1) * SPAN, 0)
                mstat[span, cols] = top
                lstat[span, cols] = total
                oacc[span, cols] = mixed
        for c in reversed(range(spans)):
            span = slice(c * SPAN, (c + 1) * SPAN)
            rows_copy(layer, c).wait_recv()
            for k in range(0, 2 * ATTN, 256):
                kvp[span, k : k + 256] = mm(arecv[layer, span, :], wm[layer, :, k : k + 256]).astype(BF16)
            for p in range(ATTN // LANES):
                cols = slice(p * LANES, (p + 1) * LANES)
                top, total, mixed = attend(p, span, kvp, c * SPAN, rows, rows)
                top0 = mstat[span, cols]
                most = jnp.maximum(top, top0)
                wa, wb = jnp.exp(top0 - most), jnp.exp(top - most)
                inv = 1.0 / (wa * lstat[span, cols] + wb * total)
                gbuf[span, cols] = ((wa * oacc[span, cols] + wb * mixed) * inv).astype(BF16)
        weight_copy(layer, 4).wait()
        att = gbuf[:, 0:ATTN]
        for c in range(0, width, 256):
            out_ref[:, c : c + 256] = hid[:, c : c + 256] + mm(att, wg[layer, :, c : c + 256])
        tail_copy(layer).wait_send()
        for c in range(spans):
            rows_copy(layer, c).wait_send()
        for k in range(team):
            unless_me(k, lambda: gather_copy(layer, k, lid).wait_send())
            unless_me(k, lambda: return_copy(layer, k, lid).wait_send())

        @pl.when(mine_team < teams - 1)
        def _():
            chain_copy(layer).wait_send()

        return carry

    lax.fori_loop(0, LAYERS, block, 0)


def shards(
    n, latents, timestep, lookback, modulation, input_weight, step_weight, conv_weight, step_bias,
    decay_log, skip_gain, norm_gain, output_weight, query_weight, memory_weight, merge_weight,
):
    frames_dev, tok, width = latents.shape
    rows = frames_dev * tok
    assert n % PAIRS == 0
    vmem = pl.BlockSpec(memory_space=pltpu.VMEM)
    smem = pl.BlockSpec(memory_space=pltpu.SMEM)
    hbm = pl.BlockSpec(memory_space=pl.ANY)
    mixed_cols = INNER + 2 * STATE
    dma = pltpu.SemaphoreType.DMA
    out = pl.pallas_call(
        functools.partial(kernel, n),
        out_shape=jax.ShapeDtypeStruct((rows, width), F32),
        in_specs=[
            vmem, smem, smem, vmem, hbm, vmem, vmem, vmem, vmem, vmem, vmem, hbm, hbm, hbm, hbm,
        ],
        out_specs=vmem,
        scratch_shapes=[
            pltpu.VMEM(input_weight.shape, BF16),
            pltpu.VMEM(output_weight.shape, BF16),
            pltpu.VMEM(query_weight.shape, BF16),
            pltpu.VMEM(memory_weight.shape, BF16),
            pltpu.VMEM(merge_weight.shape, BF16),
            dma((LAYERS, 5)),
            pltpu.VMEM((rows, width), F32),
            pltpu.VMEM((rows, width), BF16),
            pltpu.VMEM((rows, INNER), BF16),
            pltpu.VMEM((rows + 8, mixed_cols), F32),
            pltpu.VMEM((rows, mixed_cols), BF16),
            pltpu.VMEM((rows, INNER), F32),
            pltpu.VMEM((rows, INNER), BF16),
            pltpu.VMEM((SPAN, SPAN), F32),
            pltpu.VMEM((LANES, INNER), BF16),
            pltpu.VMEM((rows, 2 * rows), F32),
            pltpu.VMEM((LANES, LANES), BF16),
            pltpu.VMEM((LAYERS, PAIRS, STATE + 16, LANES), BF16),
            pltpu.VMEM((LAYERS, PAIRS, STATE + 16, LANES), BF16),
            pltpu.VMEM((LAYERS, PAIRS, STATE, LANES), BF16),
            pltpu.VMEM((LAYERS, PAIRS, STATE, LANES), BF16),
            dma((LAYERS, PAIRS)), dma((LAYERS, PAIRS)), dma((LAYERS, PAIRS)), dma((LAYERS, PAIRS)),
            pltpu.VMEM((LAYERS, STATE, LANES), BF16),
            pltpu.VMEM((LAYERS, STATE, LANES), BF16),
            dma((LAYERS,)), dma((LAYERS,)),
            pltpu.VMEM((LAYERS, 16, mixed_cols), BF16),
            pltpu.VMEM((LAYERS, 16, mixed_cols), BF16),
            dma((LAYERS,)), dma((LAYERS,)),
            pltpu.VMEM((LAYERS, rows, width), BF16),
            pltpu.VMEM((LAYERS, rows, width), BF16),
            dma((LAYERS, rows // SPAN)), dma((LAYERS, rows // SPAN)),
            pltpu.VMEM((rows, ATTN), BF16),
            pltpu.VMEM((rows, 2 * ATTN), BF16),
            pltpu.VMEM((rows, 2 * ATTN), BF16),
            pltpu.VMEM((rows, ATTN), F32),
            pltpu.VMEM((rows, ATTN), F32),
            pltpu.VMEM((rows, ATTN), F32),
            pltpu.VMEM((rows, INNER), F32),
            pltpu.VMEM((rows, INNER), F32),
        ],
        compiler_params=pltpu.CompilerParams(
            collective_id=0, has_side_effects=True, vmem_limit_bytes=56 * 1024 * 1024
        ),
    )(
        latents.reshape(rows, width), timestep, lookback, modulation, input_weight,
        jnp.swapaxes(step_weight, 1, 2), conv_weight, jnp.swapaxes(step_bias, 1, 2), decay_log, skip_gain, norm_gain, output_weight, query_weight,
        memory_weight, merge_weight,
    )
    return out.reshape(latents.shape)


def solution(mesh):
    split = P(("groups", "frames"))
    frames = P(("groups", "frames"), None, None)
    return jax.shard_map(
        functools.partial(shards, mesh.shape["frames"]),
        mesh=mesh,
        in_specs=(frames, split, split) + (P(),) * 12,
        out_specs=frames,
        check_vma=False,
    )
```

```python
import functools

import jax
import jax.numpy as jnp
from jax import lax
from jax.experimental import pallas as pl
from jax.experimental.pallas import tpu as pltpu
from jax.sharding import PartitionSpec as P

HEADS = 16
HEAD_DIM = 64
STATE = 128
ATT_HEADS = 8
LAYERS = 2
CONV = 4
SPAN = 128
WINDOW = 8
EPS = 1e-06
HEAD_EPS = 1e-05
LANES = 128
INNER = HEADS * HEAD_DIM
ATTN = ATT_HEADS * HEAD_DIM
PAIRS = INNER // LANES
F32 = jnp.float32
BF16 = jnp.bfloat16
HIGH = lax.Precision.HIGHEST
MESH = pl.DeviceIdType.MESH


def mm(a, b):
    return jnp.dot(a, b, preferred_element_type=F32)


def mm_t(a, b):
    return lax.dot_general(a, b, (((1,), (1,)), ((), ())), preferred_element_type=F32)


def sigmoid(x):
    return 0.5 * jnp.tanh(0.5 * x) + 0.5


def iota(shape, dim):
    return lax.broadcasted_iota(jnp.int32, shape, dim)


def kernel(
    n,
    x_ref, ts_ref, lb_ref, mod_ref, win_hbm, ws_ref, conv_ref, sbias_ref, dlog_ref, skip_ref,
    gain_ref, wout_hbm, wq_hbm, wm_hbm, wg_hbm,
    out_ref,
    win, wout, wq, wm, wg, wsem,
    hid, ubuf, gate, ext, act, yloc, gbuf, tri, expand, bias, ones,
    s1, r1, s2, r2, s1s, s1r, s2s, s2r, cin, cout, cs, cr,
    tsend, trecv, tss, tsr, asend, arecv, ass, asr,
    qb, kv, kvp, oacc, mstat, lstat, swish, growx,
):
    rows, width = x_ref.shape
    spans = rows // SPAN
    tok = rows // WINDOW
    me = lax.axis_index("frames")
    team = PAIRS
    teams = n // team
    mine_team = me // team
    lid = lax.rem(me, team)
    base_id = mine_team * team
    nxt = lax.rem(me + 1, n)
    ts = ts_ref[0]

    def weight_copy(layer, k):
        src, dst = ((win_hbm, win), (wout_hbm, wout), (wq_hbm, wq), (wm_hbm, wm), (wg_hbm, wg))[k]
        return pltpu.make_async_copy(src.at[layer], dst.at[layer], wsem.at[layer, k])

    for layer in range(LAYERS):
        for k in range(5):
            weight_copy(layer, k).start()

    barrier = pltpu.get_barrier_semaphore()

    def greet(k, c):
        pl.semaphore_signal(
            barrier, inc=1, device_id={"frames": lax.rem(me + k, n)}, device_id_type=MESH
        )
        return c

    lax.fori_loop(1, n, greet, 0)

    out_ref[...] = x_ref[...].astype(F32)
    tri[...] = jnp.where(iota((SPAN, SPAN), 0) >= iota((SPAN, SPAN), 1), 1.0, 0.0).astype(F32)
    lane_k = iota((LANES, INNER), 0)
    lane_j = iota((LANES, INNER), 1)
    expand[...] = jnp.where(
        (lane_k < 3 * HEADS) & (lax.rem(lane_k, HEADS) == lane_j // HEAD_DIM), 1.0, 0.0
    ).astype(BF16)
    half_a = iota((LANES, LANES), 0) // HEAD_DIM
    half_b = iota((LANES, LANES), 1) // HEAD_DIM
    ones[...] = jnp.where(half_a == half_b, 1.0, 0.0).astype(BF16)
    key_col = iota((tok, rows), 1) // tok
    for f in range(WINDOW):
        reach = lb_ref[f]
        own = (key_col <= f) & (key_col >= f - reach)
        prev = (key_col - WINDOW >= f - reach) & (me > 0)
        bias[f * tok : (f + 1) * tok, 0:rows] = jnp.where(own, 0.0, -1e30)
        bias[f * tok : (f + 1) * tok, rows : 2 * rows] = jnp.where(prev, 0.0, -1e30)
    spread = jnp.where(
        iota((HEADS, LANES), 0) == lax.rem(iota((HEADS, LANES), 1), HEADS), 1.0, 0.0
    ).astype(F32)

    def widen(x):
        group = iota(x.shape, 1) // HEADS
        hi = x.astype(BF16).astype(F32)
        rest = x - hi
        mid = rest.astype(BF16).astype(F32)
        low = rest - mid
        packed = jnp.where(group == 0, hi, jnp.where(group == 1, mid, jnp.where(group == 2, low, 0.0)))
        return packed.astype(BF16)

    def repeat_heads(row):
        return jnp.dot(row, spread, precision=HIGH, preferred_element_type=F32)

    def modulate(src, dst, shift, scale, which):
        for c in which:
            v = src[c * SPAN : (c + 1) * SPAN, :]
            inv = lax.rsqrt(jnp.mean(v * v, axis=-1, keepdims=True) + EPS)
            dst[c * SPAN : (c + 1) * SPAN, :] = ((v * inv) * (1.0 + scale) + shift).astype(BF16)

    def tail_copy(layer):
        return pltpu.make_async_remote_copy(
            src_ref=tsend.at[layer], dst_ref=trecv.at[layer], send_sem=tss.at[layer],
            recv_sem=tsr.at[layer], device_id={"frames": nxt}, device_id_type=MESH,
        )

    def rows_copy(layer, c):
        span = pl.ds(c * SPAN, SPAN)
        return pltpu.make_async_remote_copy(
            src_ref=asend.at[layer, span], dst_ref=arecv.at[layer, span], send_sem=ass.at[layer, c],
            recv_sem=asr.at[layer, c], device_id={"frames": nxt}, device_id_type=MESH,
        )

    def gather_copy(layer, owner, slot):
        return pltpu.make_async_remote_copy(
            src_ref=s1.at[layer, owner], dst_ref=r1.at[layer, slot], send_sem=s1s.at[layer, owner],
            recv_sem=s1r.at[layer, slot], device_id={"frames": base_id + owner}, device_id_type=MESH,
        )

    def return_copy(layer, to, slot):
        return pltpu.make_async_remote_copy(
            src_ref=s2.at[layer, to], dst_ref=r2.at[layer, slot], send_sem=s2s.at[layer, to],
            recv_sem=s2r.at[layer, slot], device_id={"frames": base_id + to}, device_id_type=MESH,
        )

    def chain_copy(layer):
        return pltpu.make_async_remote_copy(
            src_ref=cout.at[layer], dst_ref=cin.at[layer], send_sem=cs.at[layer],
            recv_sem=cr.at[layer], device_id={"frames": lax.rem(me + team, n)}, device_id_type=MESH,
        )

    def each_mate(fn):
        def step(k, c):
            fn(lax.rem(lid + lax.rem(k + team // 2 - 2, team - 1) + 1, team))
            return c

        lax.fori_loop(1, team, step, 0)

    def unless_me(k, fn):
        @pl.when(lid != k)
        def _():
            fn()

    @pl.when(mine_team == 0)
    def _():
        cin[...] = jnp.zeros_like(cin)

    first = iota((SPAN, LANES), 1) < HEAD_DIM

    def block(layer, carry):
        mods = mod_ref[layer, ts].astype(F32)
        modulate(out_ref, ubuf, mods[0:1, :], mods[1:2, :], range(spans))
        weight_copy(layer, 0).wait()
        u = ubuf[...]
        mixed_cols = INNER + 2 * STATE
        for c in range(0, mixed_cols, 256):
            res = mm(u, win[layer, :, INNER + c : INNER + c + 256]).astype(BF16)
            ext[8 : 8 + rows, c : c + 256] = res.astype(F32)
            tsend[layer, :, c : c + 256] = res[rows - 16 :, :]

        @pl.when(layer == 0)
        def _():
            pl.semaphore_wait(barrier, n - 1)

        tail_copy(layer).start()
        for c in range(0, INNER, 256):
            gate[:, c : c + 256] = mm(u, win[layer, :, c : c + 256]).astype(BF16)
        wstep = lax.dot_general(
            spread.astype(BF16), ws_ref[layer], (((0,), (0,)), ((), ())), preferred_element_type=F32
        ).astype(BF16)
        sbias = sbias_ref[layer]
        here = jnp.where(iota(sbias.shape, 1) == ts, sbias, 0.0)
        here = jnp.sum(jnp.sum(here, axis=-1, keepdims=True) * spread, axis=0, keepdims=True)
        raw = mm_t(u, wstep) + here
        step = jnp.maximum(raw, 0.0) + jnp.log1p(jnp.exp(-jnp.abs(raw)))
        logd = -jnp.exp(repeat_heads(dlog_ref[pl.ds(layer, 1), :])) * step
        cums = [
            jnp.dot(tri[...], logd[c * SPAN : (c + 1) * SPAN, :], precision=HIGH, preferred_element_type=F32)
            for c in range(spans)
        ]
        steps = [step[c * SPAN : (c + 1) * SPAN, :] for c in range(spans)]
        taps = conv_ref[layer]
        for r in reversed(range(spans)):
            if r == 0:
                tail_copy(layer).wait_recv()
                for c in range(0, mixed_cols, 256):
                    got = trecv[layer, :, c : c + 256].astype(F32)
                    ext[0:8, c : c + 256] = jnp.where(me > 0, got[8:16, :], 0.0)
            base = 8 - (CONV - 1) + r * SPAN
            for c in range(0, mixed_cols, LANES):
                total = taps[0:1, c : c + LANES] * ext[base : base + SPAN, c : c + LANES]
                for k in range(1, CONV):
                    total = total + taps[k : k + 1, c : c + LANES] * ext[
                        base + k : base + k + SPAN, c : c + LANES
                    ]
                act[r * SPAN : (r + 1) * SPAN, c : c + LANES] = (total * sigmoid(total)).astype(BF16)
        ends = [cum[SPAN - 1 : SPAN, :] for cum in cums]
        in_map = [act[c * SPAN : (c + 1) * SPAN, INNER : INNER + STATE] for c in range(spans)]
        out_map = [act[c * SPAN : (c + 1) * SPAN, INNER + STATE :] for c in range(spans)]
        in_t = [m.astype(F32).T.astype(BF16) for m in in_map]
        edges = [widen(jnp.exp(ends[c] - cums[c]) * steps[c]) for c in range(spans)]
        end_rows = [widen(jnp.broadcast_to(jnp.exp(e), (16, LANES))) for e in ends]
        befores = []
        for p in range(PAIRS):
            cols = slice(p * LANES, (p + 1) * LANES)
            state = None
            decay = None
            for c in range(spans):
                scaled = act[c * SPAN : (c + 1) * SPAN, cols].astype(F32) * mm(edges[c], expand[:, cols])
                term = mm(in_t[c], scaled.astype(BF16))
                row = mm(end_rows[c], expand[:, cols])
                if state is None:
                    state, decay = term, row
                else:
                    gbuf[(c - 1) * SPAN : c * SPAN, cols] = state.astype(BF16)
                    state = row[0:1, :] * state + term
                    decay = row * decay
            s1[layer, p, 0:STATE, :] = state.astype(BF16)
            s1[layer, p, STATE:, :] = decay.astype(BF16)
        each_mate(lambda to: gather_copy(layer, to, lid).start())
        r1[layer, lid] = s1[layer, lid]

        lower = iota((SPAN, SPAN), 0) >= iota((SPAN, SPAN), 1)
        grow = [None] * spans
        reach_end = None
        for c in range(spans):
            span = slice(c * SPAN, (c + 1) * SPAN)
            cum, cum_t, step_t = cums[c], cums[c].T, steps[c].T
            affinity = jnp.where(lower, mm_t(out_map[c], in_map[c]), 0.0)
            inner_grow = widen(jnp.exp(cum))
            total_log = cum if reach_end is None else cum + reach_end
            grow[c] = widen(jnp.exp(total_log))
            reach_end = ends[c] if reach_end is None else reach_end + ends[c]
            for p in range(PAIRS):
                cols = slice(p * LANES, (p + 1) * LANES)
                values = act[span, cols]
                outs = []
                for h in (2 * p, 2 * p + 1):
                    gaps = jnp.minimum(cum[:, h : h + 1] - cum_t[h : h + 1, :], 0.0)
                    mixing = (affinity * jnp.exp(gaps) * step_t[h : h + 1, :]).astype(BF16)
                    outs.append(mm(mixing, values))
                y = jnp.where(first, outs[0], outs[1])
                if c > 0:
                    inner = mm(out_map[c], gbuf[(c - 1) * SPAN : c * SPAN, cols])
                    y = y + inner * mm(inner_grow, expand[:, cols])
                yloc[span, cols] = y

        run = jnp.zeros((STATE, LANES), F32)
        whole = jnp.ones((1, LANES), F32)
        for k in range(team):
            unless_me(k, lambda: gather_copy(layer, k, k).wait_recv())
            decay = r1[layer, k, STATE : STATE + 1, :].astype(F32)
            run = decay * run + r1[layer, k, 0:STATE, :].astype(F32)
            whole = whole * decay

        @pl.when(mine_team > 0)
        def _():
            chain_copy(layer).wait_recv()

        before = cin[layer].astype(F32)
        cout[layer] = (whole * before + run).astype(BF16)

        @pl.when(mine_team < teams - 1)
        def _():
            chain_copy(layer).start()

        for k in range(team):
            s2[layer, k] = before.astype(BF16)
            before = r1[layer, k, STATE : STATE + 1, :].astype(F32) * before + r1[
                layer, k, 0:STATE, :
            ].astype(F32)
        each_mate(lambda to: return_copy(layer, to, lid).start())
        r2[layer, lid] = s2[layer, lid]
        skip_row = widen(repeat_heads(jnp.broadcast_to(skip_ref[pl.ds(layer, 1), :], (16, HEADS))))
        for p in range(PAIRS):
            cols = slice(p * LANES, (p + 1) * LANES)
            skip = mm(skip_row, expand[:, cols])[0:1, :]
            for c in range(spans):
                span = slice(c * SPAN, (c + 1) * SPAN)
                yloc[span, cols] = yloc[span, cols] + skip * act[span, cols].astype(F32)
                z = gate[span, cols].astype(F32)
                swish[span, cols] = z * sigmoid(z)
                growx[span, cols] = mm(grow[c], expand[:, cols])

        gain = gain_ref[pl.ds(layer, 1), :]
        for p in range(PAIRS):
            cols = slice(p * LANES, (p + 1) * LANES)
            unless_me(p, lambda: return_copy(layer, p, p).wait_recv())
            incoming = r2[layer, p]
            for c in range(spans):
                span = slice(c * SPAN, (c + 1) * SPAN)
                carried = mm(out_map[c], incoming) * growx[span, cols]
                y = yloc[span, cols] + carried
                g = y * swish[span, cols]
                sq = g * g
                hi = sq.astype(BF16)
                lo = (sq - hi.astype(F32)).astype(BF16)
                ms = (mm(hi, ones[...]) + mm(lo, ones[...])) * (1.0 / HEAD_DIM)
                gbuf[span, cols] = (g * lax.rsqrt(ms + HEAD_EPS) * gain[:, cols]).astype(BF16)
        weight_copy(layer, 1).wait()
        for r in reversed(range(spans)):
            span = slice(r * SPAN, (r + 1) * SPAN)
            for c in range(0, width, 256):
                hid[span, c : c + 256] = out_ref[span, c : c + 256] + mm(
                    gbuf[span, :], wout[layer, :, c : c + 256]
                )
            modulate(hid, asend.at[layer], mods[2:3, :], mods[3:4, :], [r])
            rows_copy(layer, r).start()
        weight_copy(layer, 2).wait()
        weight_copy(layer, 3).wait()
        a = asend[layer]
        for c in range(0, ATTN, 256):
            q = mm(a, wq[layer, :, c : c + 256]).astype(BF16)
            qb[:, c : c + 256] = (q.astype(F32) * HEAD_DIM ** (-0.5)).astype(BF16)
        for c in range(0, 2 * ATTN, 256):
            kv[:, c : c + 256] = mm(a, wm[layer, :, c : c + 256]).astype(BF16)

        def attend(p, span, keys, lo, hi, shift):
            cols = slice(p * LANES, (p + 1) * LANES)
            q, k = qb[span, cols], keys[lo:hi, cols]
            vals = keys[lo:hi, ATTN + p * LANES : ATTN + (p + 1) * LANES]
            lanes = iota(vals.shape, 1) < HEAD_DIM
            tops, mixes = [], []
            for h in range(2):
                mine = first if h == 0 else ~first
                s = mm_t(jnp.where(mine, q, jnp.zeros_like(q)), k) + bias[span, shift + lo : shift + hi]
                top = jnp.max(s, axis=-1, keepdims=True)
                mine = lanes if h == 0 else ~lanes
                w = jnp.exp(s - top).astype(BF16)
                mixes.append(mm(w, jnp.where(mine, vals, jnp.ones_like(vals))))
                tops.append(top)
            top = jnp.where(first, tops[0], tops[1])
            total = pltpu.roll(jnp.where(first, mixes[1], mixes[0]), HEAD_DIM, 1)
            return top, total, jnp.where(first, mixes[0], mixes[1])

        for p in range(ATTN // LANES):
            cols = slice(p * LANES, (p + 1) * LANES)
            for c in range(spans):
                span = slice(c * SPAN, (c + 1) * SPAN)
                top, total, mixed = attend(p, span, kv, 0, (c + 1) * SPAN, 0)
                mstat[span, cols] = top
                lstat[span, cols] = total
                oacc[span, cols] = mixed
        for c in reversed(range(spans)):
            span = slice(c * SPAN, (c + 1) * SPAN)
            rows_copy(layer, c).wait_recv()
            for k in range(0, 2 * ATTN, 256):
                kvp[span, k : k + 256] = mm(arecv[layer, span, :], wm[layer, :, k : k + 256]).astype(BF16)
            for p in range(ATTN // LANES):
                cols = slice(p * LANES, (p + 1) * LANES)
                top, total, mixed = attend(p, span, kvp, c * SPAN, rows, rows)
                top0 = mstat[span, cols]
                most = jnp.maximum(top, top0)
                wa, wb = jnp.exp(top0 - most), jnp.exp(top - most)
                inv = 1.0 / (wa * lstat[span, cols] + wb * total)
                gbuf[span, cols] = ((wa * oacc[span, cols] + wb * mixed) * inv).astype(BF16)
        weight_copy(layer, 4).wait()
        att = gbuf[:, 0:ATTN]
        for c in range(0, width, 256):
            out_ref[:, c : c + 256] = hid[:, c : c + 256] + mm(att, wg[layer, :, c : c + 256])
        tail_copy(layer).wait_send()
        for c in range(spans):
            rows_copy(layer, c).wait_send()
        for k in range(team):
            unless_me(k, lambda: gather_copy(layer, k, lid).wait_send())
            unless_me(k, lambda: return_copy(layer, k, lid).wait_send())

        @pl.when(mine_team < teams - 1)
        def _():
            chain_copy(layer).wait_send()

        return carry

    lax.fori_loop(0, LAYERS, block, 0)


def shards(
    n, latents, timestep, lookback, modulation, input_weight, step_weight, conv_weight, step_bias,
    decay_log, skip_gain, norm_gain, output_weight, query_weight, memory_weight, merge_weight,
):
    frames_dev, tok, width = latents.shape
    rows = frames_dev * tok
    assert n % PAIRS == 0
    vmem = pl.BlockSpec(memory_space=pltpu.VMEM)
    smem = pl.BlockSpec(memory_space=pltpu.SMEM)
    hbm = pl.BlockSpec(memory_space=pl.ANY)
    mixed_cols = INNER + 2 * STATE
    dma = pltpu.SemaphoreType.DMA
    out = pl.pallas_call(
        functools.partial(kernel, n),
        out_shape=jax.ShapeDtypeStruct((rows, width), F32),
        in_specs=[
            vmem, smem, smem, vmem, hbm, vmem, vmem, vmem, vmem, vmem, vmem, hbm, hbm, hbm, hbm,
        ],
        out_specs=vmem,
        scratch_shapes=[
            pltpu.VMEM(input_weight.shape, BF16),
            pltpu.VMEM(output_weight.shape, BF16),
            pltpu.VMEM(query_weight.shape, BF16),
            pltpu.VMEM(memory_weight.shape, BF16),
            pltpu.VMEM(merge_weight.shape, BF16),
            dma((LAYERS, 5)),
            pltpu.VMEM((rows, width), F32),
            pltpu.VMEM((rows, width), BF16),
            pltpu.VMEM((rows, INNER), BF16),
            pltpu.VMEM((rows + 8, mixed_cols), F32),
            pltpu.VMEM((rows, mixed_cols), BF16),
            pltpu.VMEM((rows, INNER), F32),
            pltpu.VMEM((rows, INNER), BF16),
            pltpu.VMEM((SPAN, SPAN), F32),
            pltpu.VMEM((LANES, INNER), BF16),
            pltpu.VMEM((rows, 2 * rows), F32),
            pltpu.VMEM((LANES, LANES), BF16),
            pltpu.VMEM((LAYERS, PAIRS, STATE + 16, LANES), BF16),
            pltpu.VMEM((LAYERS, PAIRS, STATE + 16, LANES), BF16),
            pltpu.VMEM((LAYERS, PAIRS, STATE, LANES), BF16),
            pltpu.VMEM((LAYERS, PAIRS, STATE, LANES), BF16),
            dma((LAYERS, PAIRS)), dma((LAYERS, PAIRS)), dma((LAYERS, PAIRS)), dma((LAYERS, PAIRS)),
            pltpu.VMEM((LAYERS, STATE, LANES), BF16),
            pltpu.VMEM((LAYERS, STATE, LANES), BF16),
            dma((LAYERS,)), dma((LAYERS,)),
            pltpu.VMEM((LAYERS, 16, mixed_cols), BF16),
            pltpu.VMEM((LAYERS, 16, mixed_cols), BF16),
            dma((LAYERS,)), dma((LAYERS,)),
            pltpu.VMEM((LAYERS, rows, width), BF16),
            pltpu.VMEM((LAYERS, rows, width), BF16),
            dma((LAYERS, rows // SPAN)), dma((LAYERS, rows // SPAN)),
            pltpu.VMEM((rows, ATTN), BF16),
            pltpu.VMEM((rows, 2 * ATTN), BF16),
            pltpu.VMEM((rows, 2 * ATTN), BF16),
            pltpu.VMEM((rows, ATTN), F32),
            pltpu.VMEM((rows, ATTN), F32),
            pltpu.VMEM((rows, ATTN), F32),
            pltpu.VMEM((rows, INNER), F32),
            pltpu.VMEM((rows, INNER), F32),
        ],
        compiler_params=pltpu.CompilerParams(
            collective_id=0, has_side_effects=True, vmem_limit_bytes=56 * 1024 * 1024
        ),
    )(
        latents.reshape(rows, width), timestep, lookback, modulation, input_weight,
        jnp.swapaxes(step_weight, 1, 2), conv_weight, jnp.swapaxes(step_bias, 1, 2), decay_log, skip_gain, norm_gain, output_weight, query_weight,
        memory_weight, merge_weight,
    )
    return out.reshape(latents.shape)


def solution(mesh):
    split = P(("groups", "frames"))
    frames = P(("groups", "frames"), None, None)
    return jax.shard_map(
        functools.partial(shards, mesh.shape["frames"]),
        mesh=mesh,
        in_specs=(frames, split, split) + (P(),) * 12,
        out_specs=frames,
        check_vma=False,
    )
```
